32 devices in a mesh: trades: 8 (over y, x, core), paths: 4 (over z).
Axes of the slice: x: 2, y: 2, z: 4, core: 2. Of those that a mesh axis runs over, the one named last changes fastest.
Arguments:
- path_states: bfloat16 [2, 1024, 512], P(None, 'paths'), may hold values from -6 to 6
- trade_loads: bfloat16 [4096, 512], P('trades'), may hold values from -0.25 to 0.25
- trade_amounts: float32 [2, 4096], P(None, 'trades'), may hold values from -6 to 6
- trade_legs: int32 [2, 4096], P(None, 'trades'), may hold values from 0 to 39
- trade_set: int32 [4096], P('trades'), may hold values from 0 to 255, as said below
- set_slot: int32 [256], replicated, may hold values from 0 to 255, as said below
- risk_weights: float32 [40], replicated, may hold values from 0.5 to 4
Outputs:
- fitted_margin: float32 [2, 256, 1024], P(None, 'trades', 'paths')
- exposure: float32 [2, 256], P(None, 'trades')
The draws below stay inside these ranges and needn't reach their ends.
Inputs may be any that keep to these rules, and one draw needn't show every extreme that they name: `trade_set`: each row of one trade shard (aligned blocks of 512 trades) names a set; at most 160 trades of one block belong to the sets of one owner (owner = set_slot // 32), and one owner receives exactly 160 from every block. `set_slot`: A permutation of the netting sets.
All inputs are finite; a program needn't handle non-finite values.
Results may differ from the reference program's by a relative error of at most 0.0075.
Values may be sent and summed in bfloat16 or wider, within the bound.
No kernel may reach another device: no remote copies, remote signals or barrier semaphores. Data moves between devices by JAX's collectives and lax.ppermute only.
A program may use at most 64 MiB of HBM per device.

```python
import math
import jax
import jax.numpy as jnp
import numpy as np
from jax import lax

B = 40
NB = 16
K = 512
DATES = 2
T_DEV = 512
S_DEV = 32
TRADES = 4096
PATHS = 1024
SETS = 256
CAP = 160


def owner_plan(key):
    blocks = TRADES // T_DEV
    heavy_count = blocks // 4
    pool_index = np.concatenate([np.repeat(np.arange(heavy_count), CAP), heavy_count + np.repeat(np.arange(blocks - heavy_count), CAP // 4)])
    key_slot, key_full, key_rest = jax.random.split(jax.random.fold_in(key, 7), 3)
    set_slot = jax.random.permutation(key_slot, SETS).astype(jnp.int32)
    set_of_slot = jnp.zeros((SETS,), jnp.int32).at[set_slot].set(jnp.arange(SETS, dtype=jnp.int32))
    full_owner = jax.random.randint(key_full, (), 0, blocks).astype(jnp.int32)
    places = jnp.arange(blocks, dtype=jnp.int32)

    def one_block(block_key):
        key_order, key_pool, key_mix, key_within = jax.random.split(block_key, 4)
        owner_order = jax.random.permutation(key_order, blocks).astype(jnp.int32)
        full_place = jnp.sum(jnp.where(owner_order == full_owner, places, 0))
        leading = owner_order[0]
        owner_order = jnp.where(places == 0, full_owner, jnp.where(places == full_place, leading, owner_order))
        owner_pool = owner_order[pool_index]
        remainder = jax.random.permutation(key_pool, owner_pool[CAP:])
        chosen = jnp.concatenate([owner_pool[:CAP], remainder[:T_DEV - CAP]])
        chosen = jax.random.permutation(key_mix, chosen)
        within = jax.random.randint(key_within, (T_DEV,), 0, S_DEV).astype(jnp.int32)
        return set_of_slot[chosen * S_DEV + within]
    block_keys = jax.random.split(key_rest, blocks)
    trade_set = jax.vmap(one_block)(block_keys).reshape(TRADES)
    return (trade_set.astype(jnp.int32), set_slot)


def draw_trade_set(key, part):
    return owner_plan(key)[0]


def draw_set_slot(key, part):
    return owner_plan(key)[1]


def set_ends(array, own_key, smallest, largest):
    dims = array.shape
    index_at = [jax.random.randint(jax.random.fold_in(own_key, axis), (), 0, dims[axis]) for axis in range(len(dims))]
    array = array.at[tuple(index_at)].set(smallest)
    longest = dims.index(max(dims))
    index_at[longest] = (index_at[longest] + 1) % dims[longest]
    return array.at[tuple(index_at)].set(largest)


def block_scale(own_key, dims, cuts, low, high):
    factor_of = 1.0
    for axis_at, parts in cuts:
        steps = jax.random.uniform(jax.random.fold_in(jax.random.fold_in(own_key, 6), axis_at), (parts,), jnp.float32, low / len(cuts), high / len(cuts))
        factor_of = factor_of * jnp.repeat(jnp.exp(steps), dims[axis_at] // parts).reshape((-1,) + (1,) * (len(dims) - 1 - axis_at))
    return factor_of


def gaussian(own_key, extent, width, most, pieces=(), kind=jnp.bfloat16):
    entries = width * jax.random.normal(own_key, extent, jnp.float32)
    if pieces:
        entries = entries * block_scale(own_key, extent, pieces, -0.22, 0.18)
    return jnp.clip(entries, -most, most).astype(kind)


def setup_inputs(seed: int = 0) -> dict:
    streams_of = jax.random.split(jax.random.key(seed), 8)
    return {
        "path_states": gaussian(streams_of[0], (DATES, PATHS, K), 1.0, 6.0, ((1, 4),)),
        "trade_loads": gaussian(streams_of[1], (TRADES, K), K ** -0.5, 0.25, ((0, 8),)),
        "trade_amounts": gaussian(streams_of[2], (2, TRADES), 1.0, 6.0, ((1, 8),), jnp.float32),
        "trade_legs": set_ends(jax.random.randint(streams_of[3], (2, TRADES), 0, B), jax.random.fold_in(streams_of[3], 1), 0, B - 1).astype(jnp.int32),
        "trade_set": draw_trade_set(jax.random.fold_in(streams_of[7], 71), 0),
        "set_slot": draw_set_slot(jax.random.fold_in(streams_of[7], 71), 0),
        "risk_weights": jnp.clip(jnp.exp(jax.random.uniform(streams_of[6], (B,), jnp.float32, math.log(0.5), math.log(4.0))), 0.5, 4.0),
    }


CORR_LEN = 8.0
IM_SCALE = 0.2
RIDGE = 0.05
VALUE_SCALE = 4.0

def price_date(states, loadings, first_amount, second_amount):
    factor_sum = jnp.dot(loadings.astype(jnp.float32), states.T.astype(jnp.float32), preferred_element_type=jnp.float32)
    first_leg = first_amount[:, None]
    second_leg = second_amount[:, None]
    trade_value = first_leg * jax.nn.softplus(factor_sum) + second_leg * jax.nn.softplus(-factor_sum)
    rise_delta = first_leg * jax.nn.sigmoid(factor_sum)
    fall_delta = -second_leg * jax.nn.sigmoid(-factor_sum)
    return jnp.stack([trade_value, rise_delta, fall_delta], axis=1)

def bucket_margin(bucket_delta, weights):
    positions = jnp.arange(B).astype(jnp.float32)
    correlation = jnp.exp(-jnp.abs(positions[:, None] - positions[None, :]) / CORR_LEN)
    weighted = bucket_delta * weights[None, :, None]
    mixed = jnp.einsum('bc,scp->sbp', correlation, weighted, precision=lax.Precision.HIGHEST)
    return IM_SCALE * jnp.sqrt(1.0 + lax.optimization_barrier(jnp.sum(weighted * mixed, axis=1)))

def design(set_value, features):
    constant = jnp.ones_like(set_value)
    spread = jnp.broadcast_to(features.T[:, None, :], (NB - 2,) + set_value.shape)
    return jnp.concatenate([constant[None], jnp.tanh(set_value / VALUE_SCALE)[None], spread], axis=0)

def reference(path_states, trade_loads, trade_amounts, trade_legs, trade_set, set_slot, risk_weights):
    fitted_rows = []
    exposure_rows = []
    for date_index in range(DATES):
        trade_terms = price_date(path_states[date_index], trade_loads, trade_amounts[0], trade_amounts[1])
        set_value = jax.ops.segment_sum(trade_terms[:, 0], trade_set, num_segments=SETS)
        bucket_delta = jax.ops.segment_sum(trade_terms[:, 1], trade_set * B + trade_legs[0], num_segments=SETS * B)
        bucket_delta = bucket_delta + jax.ops.segment_sum(trade_terms[:, 2], trade_set * B + trade_legs[1], num_segments=SETS * B)
        margin = bucket_margin(bucket_delta.reshape(SETS, B, PATHS), risk_weights)
        features = path_states[date_index][:, :NB - 2].astype(jnp.float32)
        basis_terms = design(set_value, features)
        gram_matrix = jnp.einsum('isp,jsp->sij', basis_terms, basis_terms, precision=lax.Precision.HIGHEST)
        gram_matrix = gram_matrix + RIDGE * PATHS * jnp.eye(NB, dtype=jnp.float32)[None]
        moments = jnp.einsum('isp,sp->si', basis_terms, margin, precision=lax.Precision.HIGHEST)
        coefficients = jnp.linalg.solve(gram_matrix, moments[..., None])[..., 0]
        fitted = jnp.einsum('isp,si->sp', basis_terms, coefficients, precision=lax.Precision.HIGHEST)
        fitted_rows.append(fitted)
        exposure_rows.append(lax.optimization_barrier(jnp.sum(jnp.maximum(set_value - fitted, 0.0), axis=1)) / PATHS)
    fitted_all = jnp.stack(fitted_rows)
    exposure_all = jnp.stack(exposure_rows)
    fitted_margin = jnp.zeros_like(fitted_all).at[:, set_slot].set(fitted_all)
    exposure = jnp.zeros_like(exposure_all).at[:, set_slot].set(exposure_all)
    return (fitted_margin, exposure)
```

```python
import math

import jax
import jax.numpy as jnp
from jax import lax
from jax.experimental import pallas as pl
from jax.experimental.pallas import tpu as pltpu
from jax.sharding import PartitionSpec as P

B = 40
NB = 16
DATES = 2
NF = NB - 2
META = 8
HALF = 256

CORR_LEN = 8.0
IM_SCALE = 0.2
RIDGE = 0.05
VALUE_SCALE = 4.0

F32 = jnp.float32
BF16 = jnp.bfloat16
VMEM_LIMIT = 56 << 20
NT = (((1,), (1,)), ((), ()))


def iota(shape, axis):
    return lax.broadcasted_iota(jnp.int32, shape, axis)


def dot(a, b):
    return jnp.dot(a, b, preferred_element_type=F32)


def dot_nt(a, b):
    return lax.dot_general(a, b, NT, preferred_element_type=F32)


def pieces(x, count):
    out = []
    for _ in range(count):
        piece = x.astype(BF16)
        out.append(piece)
        x = x - piece.astype(F32)
    return out


def pick_rows(rows, height):
    width = rows[0].shape[1]
    at = iota((height, width), 0)
    out = jnp.zeros((height, width), F32)
    for i, row in enumerate(rows):
        out = jnp.where(at == i, row, out)
    return out


def pack_kernel(owners, cap, set_count, me_ref, set_ref, slot_ref, amount_ref, leg_ref, load_ref, *outs):
    trades = set_ref.shape[1]
    sets = slot_ref.shape[1]
    slot = slot_ref[...].astype(F32)
    slot_owner = jnp.floor((slot + 0.5) * (1.0 / set_count))
    slot_local = slot - slot_owner * set_count
    digits = pick_rows([slot_owner, slot_local], 16).astype(BF16)
    member = jnp.where(iota((sets, trades), 0) == set_ref[...], 1.0, 0.0).astype(BF16)
    found = dot(digits, member)
    owner, local = found[0:1], found[1:2]
    height = -(-owners // 16) * 16
    marks = jnp.where(iota((height, trades), 0).astype(F32) == owner, 1.0, 0.0)
    ahead = jnp.where(iota((trades, trades), 0) < iota((trades, trades), 1), 1.0, 0.0).astype(BF16)
    rank = jnp.sum(dot(marks.astype(BF16), ahead) * marks, axis=0, keepdims=True)
    target = (owner * cap + rank).astype(jnp.int32) - me_ref[0] * cap
    target = jnp.where(target < 0, target + owners * cap, target)
    amounts = amount_ref[...]
    legs = leg_ref[...].astype(F32)
    meta = [p.astype(F32) for p in pieces(amounts[0:1], 3) + pieces(amounts[1:2], 3)]
    meta = pick_rows(meta + [legs[0:1], legs[1:2], local], 16).astype(BF16)
    loads = load_ref[...]
    for k in range(owners):
        place = jnp.where(iota((HALF, trades), 0) + k * cap == target, 1.0, 0.0).astype(BF16)
        moved = dot(place[:cap], loads)
        tags = dot_nt(meta, place)
        out = outs[k] if len(outs) > 1 else outs[0].at[k]
        out[0:cap, :] = moved.astype(BF16)
        out[cap : cap + META, 0:HALF] = tags[0:META].astype(BF16)
        out[cap : cap + META, HALF : 2 * HALF] = tags[META : 2 * META].astype(BF16)


def owner_kernel(owners, cap, set_count, weight_ref, state_ref, *refs):
    blocks = refs[: -7]
    out_ref, level_ref, delta_ref, terms_ref, high_ref, low_ref, place_ref = refs[-7:]
    if len(blocks) == 1:
        blocks = [blocks[0].at[k] for k in range(owners)]
    count = owners * cap
    cols = state_ref.shape[0]
    paths = cols // DATES
    states = state_ref[...]
    meta = jnp.zeros((2 * META, count), F32)
    for k in range(owners):
        tags = jnp.concatenate(
            [blocks[k][cap : cap + META, 0:HALF], blocks[k][cap : cap + META, HALF : 2 * HALF]], axis=0
        ).astype(F32)
        tags = jnp.where(iota(tags.shape, 1) < cap, tags, 0.0)
        tags = jnp.concatenate([tags, jnp.zeros((2 * META, count - HALF), F32)], axis=1)
        meta = meta + (pltpu.roll(tags, k * cap, 1) if k else tags)
    first = meta[0:1] + meta[1:2] + meta[2:3]
    second = meta[3:4] + meta[4:5] + meta[5:6]
    columns = pick_rows([first, second], 128).T
    loads = jnp.concatenate([block[0:cap, :] for block in blocks], axis=0)
    level_ref[...] = dot_nt(loads, states)
    step = 128
    for r in range(0, count, step):
        x = level_ref[r : r + step, :]
        a = columns[r : r + step, 0:1]
        c = columns[r : r + step, 1:2]
        e = jnp.exp(-jnp.abs(x))
        more = 1.0 + e
        tail = jnp.log(more)
        near = 1.0 / more
        far = e * near
        up = x >= 0.0
        value = a * (jnp.maximum(x, 0.0) + tail) + c * (jnp.maximum(-x, 0.0) + tail)
        terms_ref[r : r + step, :] = (a * jnp.where(up, near, far)).astype(BF16)
        terms_ref[count + r : count + r + step, :] = (-c * jnp.where(up, far, near)).astype(BF16)
        high = value.astype(BF16)
        high_ref[r : r + step, :] = high
        low_ref[r : r + step, :] = (value - high.astype(F32)).astype(BF16)
    in_set = jnp.where(iota((set_count, count), 0).astype(F32) == meta[8:9], 1.0, 0.0)
    for leg in range(2):
        at_leg = meta[6 + leg : 7 + leg]
        for b in range(B):
            place_ref[b * set_count : (b + 1) * set_count, leg * count : (leg + 1) * count] = (
                jnp.where(at_leg == float(b), in_set, 0.0).astype(BF16)
            )
    delta_ref[...] = dot(place_ref[...], terms_ref[...])
    in_set = in_set.astype(BF16)
    set_value = dot(in_set, high_ref[...]) + dot(in_set, low_ref[...])
    rho = math.exp(-1.0 / CORR_LEN)
    carry = jnp.zeros((set_count, cols), F32)
    quad = jnp.zeros((set_count, cols), F32)
    for b in range(B - 1, -1, -1):
        carry = rho * carry + weight_ref[b] * delta_ref[b * set_count : (b + 1) * set_count, :]
        quad = quad + (1.0 if b == 0 else 1.0 - rho * rho) * (carry * carry)
    margin = IM_SCALE * jnp.sqrt(1.0 + quad)
    spread = jnp.tanh(set_value / VALUE_SCALE)
    eye = jnp.where(iota((NB, 128), 0) == iota((NB, 128), 1), 1.0, 0.0).astype(BF16)
    basis = dot_nt(eye, states[:, 0:128])
    at = iota(basis.shape, 0)
    basis = jnp.where(at < NF, basis, jnp.where(at == NF, 1.0, 0.0))
    for d in range(DATES):
        own = slice(d * paths, (d + 1) * paths)
        t, m = spread[:, own], margin[:, own]
        rows = jnp.concatenate([t, m, t * t, t * m], axis=0)
        some = basis[:, own].astype(BF16)
        sums = sum(dot_nt(some, piece) for piece in pieces(rows, 3))
        out_ref[d * set_count : (d + 1) * set_count, :] = set_value[:, own]
        base = DATES * set_count
        out_ref[base + d * NB : base + (d + 1) * NB, :] = basis[:, own]
        base = base + DATES * NB
        width = 4 * set_count
        out_ref[base : base + NB, d * width : (d + 1) * width] = sums


def fit_kernel(groups, set_count, *refs):
    parts, (fit_ref, pos_ref) = refs[:groups], refs[groups:]
    paths = parts[0].shape[1]
    paths_all = groups * paths
    ridge = RIDGE * paths_all
    width = 4 * set_count
    base = DATES * (set_count + NB)
    rows = []
    for d in range(DATES):
        sums = sum(p[base : base + NB, d * width : (d + 1) * width] for p in parts)
        first = DATES * set_count + d * NB
        basis = jnp.concatenate([p[first : first + NB, :] for p in parts], axis=1).astype(BF16)
        values = jnp.concatenate([p[d * set_count : (d + 1) * set_count, :] for p in parts], axis=1)
        gram = dot_nt(basis, basis)
        diag = iota((NB, NB), 0) == iota((NB, NB), 1)
        gram = jnp.where(diag, gram + ridge, gram)
        right = sums
        at_g, at_r = iota(gram.shape, 0), iota(right.shape, 0)
        for j in range(NB - 1):
            inv = 1.0 / gram[j : j + 1, j : j + 1]
            col = gram[:, j : j + 1]
            row_g = gram[j : j + 1, :] * inv
            row_r = right[j : j + 1, :] * inv
            gram = jnp.where(at_g == j, row_g, gram - col * row_g)
            right = jnp.where(at_r == j, row_r, right - col * row_r)
        right = jnp.where(at_r < NB - 1, right, 0.0)
        solved = pltpu.roll(right, width - set_count, 1)
        last = sums[NF : NF + 1]
        square = pltpu.roll(last, width - 2 * set_count, 1) + ridge
        cross = pltpu.roll(last, width - 3 * set_count, 1)
        here = iota((1, width), 1) < set_count
        below = jnp.where(here, square - jnp.sum(sums * right, axis=0, keepdims=True), 1.0)
        above = cross - jnp.sum(sums * solved, axis=0, keepdims=True)
        slope = jnp.where(here, above / below, 0.0)
        coef = jnp.where(at_r < NB - 1, solved - right * slope, slope)
        coef = jnp.concatenate([coef, jnp.zeros((width - NB, width), F32)], axis=0).T
        coef = coef[0:set_count]
        linear = sum(dot(piece[:, 0:NB], basis) for piece in pieces(coef, 3))
        fitted = linear + coef[:, NB - 1 : NB] * jnp.tanh(values / VALUE_SCALE)
        fit_ref[d] = fitted[:, 0:paths]
        positive = jnp.sum(jnp.maximum(values - fitted, 0.0), axis=1, keepdims=True)
        rows.append(jnp.broadcast_to(positive * (1.0 / paths_all), (set_count, 128)))
    rows.append(jnp.zeros((128 - DATES * set_count, 128), F32))
    flat = jnp.concatenate(rows, axis=0).T
    for d in range(DATES):
        moved = pltpu.roll(flat, 128 - d * set_count, 1) if d else flat
        pos_ref[d : d + 1, :] = moved[0:1, 0:set_count]


def smem():
    return pl.BlockSpec(memory_space=pltpu.SMEM)


def vmem(count):
    return [pl.BlockSpec(memory_space=pltpu.VMEM)] * count


def params():
    return pltpu.CompilerParams(vmem_limit_bytes=VMEM_LIMIT)


def turn(x, axis, k):
    n = lax.axis_size(axis)
    return lax.ppermute(x, axis, [(i, (i + k) % n) for i in range(n)])


def on_device(
    path_states, trade_loads, trade_amounts, trade_legs, trade_set, set_slot, risk_weights
):
    owners = lax.axis_size("trades")
    groups = lax.axis_size("paths")
    trades, factors = trade_loads.shape
    sets = set_slot.shape[0]
    set_count = sets // owners
    cap = 5 * trades // (2 * owners)
    paths = path_states.shape[1]
    cols = DATES * paths
    count = owners * cap
    block = (cap + META, factors)
    few = owners <= 8
    me = lax.axis_index("trades").astype(jnp.int32)
    if few:
        shape = [jax.ShapeDtypeStruct(block, BF16)] * owners
    else:
        me = jnp.zeros_like(me)
        shape = [jax.ShapeDtypeStruct((owners,) + block, BF16)]
    packed = pl.pallas_call(
        lambda *refs: pack_kernel(owners, cap, set_count, *refs),
        out_shape=shape,
        in_specs=[smem()] + vmem(5),
        out_specs=vmem(len(shape)),
        compiler_params=params(),
        name="pack",
    )(
        me.reshape(1),
        trade_set.reshape(1, trades),
        set_slot.reshape(1, sets),
        trade_amounts,
        trade_legs,
        trade_loads,
    )
    if few:
        got = [packed[0]] + [turn(packed[k], "trades", k) for k in range(1, owners)]
    else:
        got = [lax.all_to_all(packed[0], "trades", split_axis=0, concat_axis=0, tiled=True)]
    packet = (DATES * (set_count + NB) + NB, paths)
    mine = pl.pallas_call(
        lambda *refs: owner_kernel(owners, cap, set_count, *refs),
        out_shape=jax.ShapeDtypeStruct(packet, F32),
        in_specs=[smem()] + vmem(1 + len(got)),
        out_specs=vmem(1)[0],
        scratch_shapes=[
            pltpu.VMEM((count, cols), F32),
            pltpu.VMEM((B * set_count, cols), F32),
            pltpu.VMEM((2 * count, cols), BF16),
            pltpu.VMEM((count, cols), BF16),
            pltpu.VMEM((count, cols), BF16),
            pltpu.VMEM((B * set_count, 2 * count), BF16),
        ],
        compiler_params=params(),
        name="owner",
    )(risk_weights, path_states.reshape(cols, factors), *got)
    parts = [mine] + [turn(mine, "paths", k) for k in range(1, groups)]
    fitted_margin, exposure = pl.pallas_call(
        lambda *refs: fit_kernel(groups, set_count, *refs),
        out_shape=[
            jax.ShapeDtypeStruct((DATES, set_count, paths), F32),
            jax.ShapeDtypeStruct((DATES, set_count), F32),
        ],
        in_specs=vmem(groups),
        out_specs=vmem(2),
        compiler_params=params(),
        name="fit",
    )(*parts)
    return (fitted_margin, exposure)


def solution(mesh):
    in_specs = (
        P(None, "paths", None),
        P("trades", None),
        P(None, "trades"),
        P(None, "trades"),
        P("trades"),
        P(),
        P(),
    )
    out_specs = (P(None, "trades", "paths"), P(None, "trades"))
    return jax.shard_map(
        on_device, mesh=mesh, in_specs=in_specs, out_specs=out_specs, check_vma=False
    )
```

```python
import math

import jax
import jax.numpy as jnp
from jax import lax
from jax.experimental import pallas as pl
from jax.experimental.pallas import tpu as pltpu
from jax.sharding import PartitionSpec as P

B = 40
NB = 16
DATES = 2
NF = NB - 2
META = 8
HALF = 256

CORR_LEN = 8.0
IM_SCALE = 0.2
RIDGE = 0.05
VALUE_SCALE = 4.0

F32 = jnp.float32
BF16 = jnp.bfloat16
VMEM_LIMIT = 56 << 20
NT = (((1,), (1,)), ((), ()))


def iota(shape, axis):
    return lax.broadcasted_iota(jnp.int32, shape, axis)


def dot(a, b):
    return jnp.dot(a, b, preferred_element_type=F32)


def dot_nt(a, b):
    return lax.dot_general(a, b, NT, preferred_element_type=F32)


def pieces(x, count):
    out = []
    for _ in range(count):
        piece = x.astype(BF16)
        out.append(piece)
        x = x - piece.astype(F32)
    return out


def pick_rows(rows, height):
    width = rows[0].shape[1]
    at = iota((height, width), 0)
    out = jnp.zeros((height, width), F32)
    for i, row in enumerate(rows):
        out = jnp.where(at == i, row, out)
    return out


def pack_kernel(owners, cap, set_count, me_ref, set_ref, slot_ref, amount_ref, leg_ref, load_ref, *outs):
    trades = set_ref.shape[1]
    sets = slot_ref.shape[1]
    slot = slot_ref[...].astype(F32)
    slot_owner = jnp.floor((slot + 0.5) * (1.0 / set_count))
    slot_local = slot - slot_owner * set_count
    digits = pick_rows([slot_owner, slot_local], 16).astype(BF16)
    member = jnp.where(iota((sets, trades), 0) == set_ref[...], 1.0, 0.0).astype(BF16)
    found = dot(digits, member)
    owner, local = found[0:1], found[1:2]
    height = -(-owners // 16) * 16
    marks = jnp.where(iota((height, trades), 0).astype(F32) == owner, 1.0, 0.0)
    ahead = jnp.where(iota((trades, trades), 0) < iota((trades, trades), 1), 1.0, 0.0).astype(BF16)
    rank = jnp.sum(dot(marks.astype(BF16), ahead) * marks, axis=0, keepdims=True)
    target = (owner * cap + rank).astype(jnp.int32) - me_ref[0] * cap
    target = jnp.where(target < 0, target + owners * cap, target)
    amounts = amount_ref[...]
    legs = leg_ref[...].astype(F32)
    meta = [p.astype(F32) for p in pieces(amounts[0:1], 3) + pieces(amounts[1:2], 3)]
    meta = pick_rows(meta + [legs[0:1], legs[1:2], local], 16).astype(BF16)
    loads = load_ref[...]
    for k in range(owners):
        place = jnp.where(iota((HALF, trades), 0) + k * cap == target, 1.0, 0.0).astype(BF16)
        moved = dot(place[:cap], loads)
        tags = dot_nt(meta, place)
        out = outs[k] if len(outs) > 1 else outs[0].at[k]
        out[0:cap, :] = moved.astype(BF16)
        out[cap : cap + META, 0:HALF] = tags[0:META].astype(BF16)
        out[cap : cap + META, HALF : 2 * HALF] = tags[META : 2 * META].astype(BF16)


def owner_kernel(owners, cap, set_count, weight_ref, state_ref, *refs):
    blocks = refs[:-8]
    out_ref, value_ref, level_ref, delta_ref, terms_ref, high_ref, low_ref, place_ref = refs[-8:]
    if len(blocks) == 1:
        blocks = [blocks[0].at[k] for k in range(owners)]
    count = owners * cap
    cols = state_ref.shape[0]
    paths = cols // DATES
    states = state_ref[...]
    meta = jnp.zeros((2 * META, count), F32)
    for k in range(owners):
        tags = jnp.concatenate(
            [blocks[k][cap : cap + META, 0:HALF], blocks[k][cap : cap + META, HALF : 2 * HALF]], axis=0
        ).astype(F32)
        tags = jnp.where(iota(tags.shape, 1) < cap, tags, 0.0)
        tags = jnp.concatenate([tags, jnp.zeros((2 * META, count - HALF), F32)], axis=1)
        meta = meta + (pltpu.roll(tags, k * cap, 1) if k else tags)
    first = meta[0:1] + meta[1:2] + meta[2:3]
    second = meta[3:4] + meta[4:5] + meta[5:6]
    columns = pick_rows([first, second], 128).T
    loads = jnp.concatenate([block[0:cap, :] for block in blocks], axis=0)
    level_ref[...] = dot_nt(loads, states)
    step = 128
    for r in range(0, count, step):
        x = level_ref[r : r + step, :]
        a = columns[r : r + step, 0:1]
        c = columns[r : r + step, 1:2]
        e = jnp.exp(-jnp.abs(x))
        more = 1.0 + e
        tail = jnp.log(more)
        near = 1.0 / more
        far = e * near
        up = x >= 0.0
        value = a * (jnp.maximum(x, 0.0) + tail) + c * (jnp.maximum(-x, 0.0) + tail)
        terms_ref[r : r + step, :] = (a * jnp.where(up, near, far)).astype(BF16)
        terms_ref[count + r : count + r + step, :] = (-c * jnp.where(up, far, near)).astype(BF16)
        high = value.astype(BF16)
        high_ref[r : r + step, :] = high
        low_ref[r : r + step, :] = (value - high.astype(F32)).astype(BF16)
    in_set = jnp.where(iota((set_count, count), 0).astype(F32) == meta[8:9], 1.0, 0.0)
    for leg in range(2):
        at_leg = meta[6 + leg : 7 + leg]
        for b in range(B):
            place_ref[b * set_count : (b + 1) * set_count, leg * count : (leg + 1) * count] = (
                jnp.where(at_leg == float(b), in_set, 0.0).astype(BF16)
            )
    delta_ref[...] = dot(place_ref[...], terms_ref[...])
    in_set = in_set.astype(BF16)
    set_value = dot(in_set, high_ref[...]) + dot(in_set, low_ref[...])
    rho = math.exp(-1.0 / CORR_LEN)
    carry = jnp.zeros((set_count, cols), F32)
    quad = jnp.zeros((set_count, cols), F32)
    for b in range(B - 1, -1, -1):
        carry = rho * carry + weight_ref[b] * delta_ref[b * set_count : (b + 1) * set_count, :]
        quad = quad + (1.0 if b == 0 else 1.0 - rho * rho) * (carry * carry)
    margin = IM_SCALE * jnp.sqrt(1.0 + quad)
    spread = jnp.tanh(set_value / VALUE_SCALE)
    eye = jnp.where(iota((NB, 128), 0) == iota((NB, 128), 1), 1.0, 0.0).astype(BF16)
    basis = dot_nt(eye, states[:, 0:128])
    at = iota(basis.shape, 0)
    basis = jnp.where(at < NF, basis, jnp.where(at == NF, 1.0, 0.0))
    sums = []
    for d in range(DATES):
        own = slice(d * paths, (d + 1) * paths)
        t, m = spread[:, own], margin[:, own]
        rows = jnp.concatenate([t, m, t * t, t * m], axis=0)
        some = basis[:, own].astype(BF16)
        sums.append(sum(dot_nt(some, piece) for piece in pieces(rows, 3)))
        value_ref[d] = set_value[:, own]
        out_ref[d * set_count : (d + 1) * set_count, :] = set_value[:, own].astype(BF16)
        base = DATES * set_count
        out_ref[base + d * NB : base + (d + 1) * NB, :] = some
    base = DATES * (set_count + NB)
    for i, piece in enumerate(pieces(jnp.concatenate(sums, axis=1), 3)):
        out_ref[base + i * NB : base + (i + 1) * NB, :] = piece


def fit_kernel(groups, set_count, value_ref, *refs):
    parts, (fit_ref, pos_ref) = refs[:groups], refs[groups:]
    paths = parts[0].shape[1]
    paths_all = groups * paths
    ridge = RIDGE * paths_all
    width = 4 * set_count
    base = DATES * (set_count + NB)
    total = sum(p[base + i * NB : base + (i + 1) * NB, :].astype(F32) for i in range(3) for p in parts)
    shape = (NB, width)
    row, lane = iota(shape, 0), iota(shape, 1)
    shift = 2 * set_count
    bases, sums, works = [], [], []
    for d in range(DATES):
        first = DATES * set_count + d * NB
        basis = jnp.concatenate([p[first : first + NB, :] for p in parts], axis=1)
        blank = jnp.zeros((shift, basis.shape[1]), BF16)
        placed = jnp.concatenate([blank, basis, blank[: width - shift - NB]], axis=0)
        gram = dot_nt(basis, placed)
        gram = jnp.where(lane - shift == row, gram + ridge, gram)
        part = total[:, d * width : (d + 1) * width]
        bases.append(basis)
        sums.append(part)
        works.append(jnp.where(lane < shift, part, gram))
    for j in range(NB - 1):
        for d in range(DATES):
            work = works[d]
            col = jnp.broadcast_to(work[:, shift + j : shift + j + 1], shape)
            inv = 1.0 / jnp.broadcast_to(col[j : j + 1, :], shape)
            pivot = jnp.broadcast_to(work[j : j + 1, :], shape) * inv
            works[d] = jnp.where(row == j, pivot, work - col * pivot)
    flats = []
    for d in range(DATES):
        part, basis = sums[d], bases[d]
        right = jnp.where(row < NB - 1, works[d], 0.0)
        solved = pltpu.roll(right, width - set_count, 1)
        last = part[NF : NF + 1]
        square = pltpu.roll(last, width - 2 * set_count, 1) + ridge
        cross = pltpu.roll(last, width - 3 * set_count, 1)
        here = iota((1, width), 1) < set_count
        below = jnp.where(here, square - jnp.sum(part * right, axis=0, keepdims=True), 1.0)
        above = cross - jnp.sum(part * solved, axis=0, keepdims=True)
        slope = jnp.where(here, above / below, 0.0)
        coef = jnp.where(row < NB - 1, solved - right * slope, slope)
        coef = jnp.concatenate([coef, jnp.zeros((width - NB, width), F32)], axis=0).T
        coef = coef[0:set_count]
        values = [value_ref[d]] + [p[d * set_count : (d + 1) * set_count, :].astype(F32) for p in parts[1:]]
        values = jnp.concatenate(values, axis=1)
        linear = sum(dot(piece[:, 0:NB], basis) for piece in pieces(coef, 3))
        fitted = linear + coef[:, NB - 1 : NB] * jnp.tanh(values * (1.0 / VALUE_SCALE))
        fit_ref[d] = fitted[:, 0:paths]
        positive = jnp.sum(jnp.maximum(values - fitted, 0.0), axis=1, keepdims=True)
        flats.append(jnp.broadcast_to(positive * (1.0 / paths_all), (set_count, 128)))
    flats.append(jnp.zeros((128 - DATES * set_count, 128), F32))
    flat = jnp.concatenate(flats, axis=0).T
    for d in range(DATES):
        moved = pltpu.roll(flat, 128 - d * set_count, 1) if d else flat
        pos_ref[d : d + 1, :] = moved[0:1, 0:set_count]


def smem():
    return pl.BlockSpec(memory_space=pltpu.SMEM)


def vmem(count):
    return [pl.BlockSpec(memory_space=pltpu.VMEM)] * count


def params():
    return pltpu.CompilerParams(vmem_limit_bytes=VMEM_LIMIT)


def turn(x, axis, k):
    n = lax.axis_size(axis)
    return lax.ppermute(x, axis, [(i, (i + k) % n) for i in range(n)])


def on_device(
    path_states, trade_loads, trade_amounts, trade_legs, trade_set, set_slot, risk_weights
):
    owners = lax.axis_size("trades")
    groups = lax.axis_size("paths")
    trades, factors = trade_loads.shape
    sets = set_slot.shape[0]
    set_count = sets // owners
    cap = 5 * trades // (2 * owners)
    paths = path_states.shape[1]
    cols = DATES * paths
    count = owners * cap
    block = (cap + META, factors)
    few = owners <= 8
    me = lax.axis_index("trades").astype(jnp.int32)
    if few:
        shape = [jax.ShapeDtypeStruct(block, BF16)] * owners
    else:
        me = jnp.zeros_like(me)
        shape = [jax.ShapeDtypeStruct((owners,) + block, BF16)]
    packed = pl.pallas_call(
        lambda *refs: pack_kernel(owners, cap, set_count, *refs),
        out_shape=shape,
        in_specs=[smem()] + vmem(5),
        out_specs=vmem(len(shape)),
        compiler_params=params(),
        name="pack",
    )(
        me.reshape(1),
        trade_set.reshape(1, trades),
        set_slot.reshape(1, sets),
        trade_amounts,
        trade_legs,
        trade_loads,
    )
    if few:
        got = [packed[0]] + [turn(packed[k], "trades", k) for k in range(1, owners)]
    else:
        got = [lax.all_to_all(packed[0], "trades", split_axis=0, concat_axis=0, tiled=True)]
    packet = (DATES * (set_count + NB) + 3 * NB, paths)
    mine, value = pl.pallas_call(
        lambda *refs: owner_kernel(owners, cap, set_count, *refs),
        out_shape=[
            jax.ShapeDtypeStruct(packet, BF16),
            jax.ShapeDtypeStruct((DATES, set_count, paths), F32),
        ],
        in_specs=[smem()] + vmem(1 + len(got)),
        out_specs=vmem(2),
        scratch_shapes=[
            pltpu.VMEM((count, cols), F32),
            pltpu.VMEM((B * set_count, cols), F32),
            pltpu.VMEM((2 * count, cols), BF16),
            pltpu.VMEM((count, cols), BF16),
            pltpu.VMEM((count, cols), BF16),
            pltpu.VMEM((B * set_count, 2 * count), BF16),
        ],
        compiler_params=params(),
        name="owner",
    )(risk_weights, path_states.reshape(cols, factors), *got)
    parts = [mine] + [turn(mine, "paths", k) for k in range(1, groups)]
    fitted_margin, exposure = pl.pallas_call(
        lambda *refs: fit_kernel(groups, set_count, *refs),
        out_shape=[
            jax.ShapeDtypeStruct((DATES, set_count, paths), F32),
            jax.ShapeDtypeStruct((DATES, set_count), F32),
        ],
        in_specs=vmem(1 + groups),
        out_specs=vmem(2),
        compiler_params=params(),
        name="fit",
    )(value, *parts)
    return (fitted_margin, exposure)


def solution(mesh):
    in_specs = (
        P(None, "paths", None),
        P("trades", None),
        P(None, "trades"),
        P(None, "trades"),
        P("trades"),
        P(),
        P(),
    )
    out_specs = (P(None, "trades", "paths"), P(None, "trades"))
    return jax.shard_map(
        on_device, mesh=mesh, in_specs=in_specs, out_specs=out_specs, check_vma=False
    )
```

```python
import math

import jax
import jax.numpy as jnp
from jax import lax
from jax.experimental import pallas as pl
from jax.experimental.pallas import tpu as pltpu
from jax.sharding import PartitionSpec as P

B = 40
NB = 16
DATES = 2
NF = NB - 2
META = 8
EARLY = 4
STEP = 8
HALF = 256

CORR_LEN = 8.0
IM_SCALE = 0.2
RIDGE = 0.05
VALUE_SCALE = 4.0

F32 = jnp.float32
BF16 = jnp.bfloat16
VMEM_LIMIT = 56 << 20
NT = (((1,), (1,)), ((), ()))


def iota(shape, axis):
    return lax.broadcasted_iota(jnp.int32, shape, axis)


def dot(a, b):
    return jnp.dot(a, b, preferred_element_type=F32)


def dot_nt(a, b):
    return lax.dot_general(a, b, NT, preferred_element_type=F32)


def pieces(x, count):
    out = []
    for _ in range(count):
        piece = x.astype(BF16)
        out.append(piece)
        x = x - piece.astype(F32)
    return out


def pick_rows(rows, height):
    width = rows[0].shape[1]
    at = iota((height, width), 0)
    out = jnp.zeros((height, width), F32)
    for i, row in enumerate(rows):
        out = jnp.where(at == i, row, out)
    return out


def pack_kernel(owners, cap, set_count, me_ref, set_ref, slot_ref, amount_ref, leg_ref, load_ref, *outs):
    trades = set_ref.shape[1]
    sets = slot_ref.shape[1]
    slot = slot_ref[...].astype(F32)
    slot_owner = jnp.floor((slot + 0.5) * (1.0 / set_count))
    slot_local = slot - slot_owner * set_count
    digits = pick_rows([slot_owner, slot_local], 16).astype(BF16)
    member = jnp.where(iota((sets, trades), 0) == set_ref[...], 1.0, 0.0).astype(BF16)
    found = dot(digits, member)
    owner, local = found[0:1], found[1:2]
    height = -(-owners // 16) * 16
    marks = jnp.where(iota((height, trades), 0).astype(F32) == owner, 1.0, 0.0)
    ahead = jnp.where(iota((trades, trades), 0) < iota((trades, trades), 1), 1.0, 0.0).astype(BF16)
    rank = jnp.sum(dot(marks.astype(BF16), ahead) * marks, axis=0, keepdims=True)
    target = (owner * cap + rank).astype(jnp.int32)
    amounts = amount_ref[...]
    legs = leg_ref[...].astype(F32)
    meta = [p.astype(F32) for p in pieces(amounts[0:1], 3) + pieces(amounts[1:2], 3)]
    meta = pick_rows(meta + [legs[0:1], legs[1:2], local], 16).astype(BF16)
    group = 8 if owners > 8 else owners
    for base in range(0, owners, group):
        chosen, places = range(base, base + group), []
        for k in chosen:
            spot = target - (me_ref[0] ^ k) * cap
            spot = jnp.where((spot >= 0) & (spot < cap), spot + (k * cap) % 128, -1)
            places.append(jnp.where(iota((HALF, trades), 0) == spot, 1.0, 0.0).astype(BF16))
        aligned = (group * cap) % 128 == 0 and cap % 16 == 0
        if aligned:
            rows = [p[(k * cap) % 128 : (k * cap) % 128 + cap] for k, p in zip(chosen, places)]
            moved = dot(jnp.concatenate(rows, axis=0), load_ref[...])
        for i, k in enumerate(chosen):
            tags = dot_nt(meta, places[i]).astype(BF16)
            out = outs[k] if len(outs) > 1 else outs[0].at[k]
            if aligned:
                out[0:cap, :] = moved[i * cap : (i + 1) * cap].astype(BF16)
            else:
                whole = dot(places[i], load_ref[...])
                out[0:cap, :] = whole[(k * cap) % 128 : (k * cap) % 128 + cap].astype(BF16)
            out[cap : cap + META, 0:HALF] = tags[0:META]
            out[cap : cap + META, HALF : 2 * HALF] = tags[META : 2 * META]


def side_by_side(blocks, at, cap, width):
    start = at * cap // 128 * 128
    tiles = [None] * (width // 128 + 2)
    for i, block in enumerate(blocks):
        first = ((at + i) * cap - start) // 128
        for j in range(HALF // 128):
            low = block[cap : cap + META, j * 128 : (j + 1) * 128]
            high = block[cap : cap + META, HALF + j * 128 : HALF + (j + 1) * 128]
            tile = jnp.concatenate([low, high], axis=0).astype(F32)
            tiles[first + j] = tile if tiles[first + j] is None else tiles[first + j] + tile
    tiles = [jnp.zeros((2 * META, 128), F32) if t is None else t for t in tiles]
    shift = at * cap - start
    if not shift:
        return jnp.concatenate(tiles[: width // 128], axis=1)
    meta = jnp.concatenate(tiles, axis=1)
    return pltpu.roll(meta, meta.shape[1] - shift, 1)[:, :width]


def price(blocks, at, cap, set_count, states, scratch):
    level_ref, terms_ref, high_ref, low_ref, place_ref = scratch
    count = len(blocks) * cap
    width = high_ref.shape[0]
    loads = jnp.concatenate([block[0:cap, :] for block in blocks], axis=0)
    level_ref[...] = dot_nt(loads, states)
    meta = side_by_side(blocks, at, cap, width)
    eye = jnp.where(iota((16, 128), 0) % 2 == iota((16, 128), 1), 1.0, 0.0).astype(BF16)
    turned = pick_rows([meta[i : i + 1] for i in (0, 3, 1, 4, 2, 5)], 16).astype(BF16)
    columns = lax.dot_general(turned, eye, (((0,), (0,)), ((), ())), preferred_element_type=F32)
    step = math.gcd(count, 128)
    for r in range(0, count, step):
        x = level_ref[r : r + step, :]
        a = columns[r : r + step, 0:1]
        c = columns[r : r + step, 1:2]
        e = jnp.exp(-jnp.abs(x))
        more = 1.0 + e
        tail = jnp.log(more)
        near = 1.0 / more
        far = e * near
        up = x >= 0.0
        value = a * (jnp.maximum(x, 0.0) + tail) + c * (jnp.maximum(-x, 0.0) + tail)
        terms_ref[r : r + step, :] = (a * jnp.where(up, near, far)).astype(BF16)
        terms_ref[width + r : width + r + step, :] = (-c * jnp.where(up, far, near)).astype(BF16)
        high = value.astype(BF16)
        high_ref[r : r + step, :] = high
        low_ref[r : r + step, :] = (value - high.astype(F32)).astype(BF16)
    if width > count:
        for ref, first in ((terms_ref, 0), (terms_ref, width), (high_ref, 0), (low_ref, 0)):
            ref[first + count : first + width, :] = jnp.zeros((width - count, ref.shape[1]), BF16)
    in_set = jnp.where(iota((set_count, width), 0).astype(F32) == meta[8:9], 1.0, 0.0)

    def bucket_deltas(first, last):
        rows = slice(first * set_count, last * set_count)
        for leg in range(2):
            for b in range(first, last):
                place_ref[b * set_count : (b + 1) * set_count, leg * width : (leg + 1) * width] = (
                    jnp.where(meta[6 + leg : 7 + leg] == float(b), in_set, 0.0).astype(BF16)
                )
        return dot(place_ref[rows, :], terms_ref[...])

    named = in_set.astype(BF16)
    return bucket_deltas, dot(named, high_ref[...]) + dot(named, low_ref[...])


def add_kernel(cap, set_count, state_ref, *refs):
    scratch, out_ref, blocks = refs[-5:], refs[-6], refs[:-6]
    deltas, value = price(blocks, 0, cap, set_count, state_ref[...], scratch)
    for b in range(0, B, STEP):
        out_ref[b * set_count : (b + STEP) * set_count, :] = deltas(b, b + STEP)
    out_ref[B * set_count :, :] = value


def owner_kernel(owners, at, cap, set_count, weight_ref, state_ref, *refs):
    out_ref, value_ref = refs[-9:-7] if at else refs[-7:-5]
    blocks = refs[1:-9] if at else refs[:-7]
    if at:
        sofar_ref, arrived = refs[-7:-5]
        fetch = pltpu.make_async_copy(refs[0], sofar_ref, arrived)
        fetch.start()
    if len(blocks) == 1 and owners > 1:
        blocks = [blocks[0].at[k] for k in range(owners)]
    cols = state_ref.shape[0]
    paths = cols // DATES
    states = state_ref[...]
    deltas, set_value = price(blocks, at, cap, set_count, states, refs[-5:])
    if at:
        fetch.wait()
        set_value = set_value + sofar_ref[B * set_count :, :]
    rho = math.exp(-1.0 / CORR_LEN)
    carry = jnp.zeros((set_count, cols), F32)
    quad = jnp.zeros((set_count, cols), F32)
    for first in range(B - STEP, -1, -STEP):
        delta = deltas(first, first + STEP)
        for b in range(first + STEP - 1, first - 1, -1):
            one = delta[(b - first) * set_count : (b - first + 1) * set_count]
            if at:
                one = one + sofar_ref[b * set_count : (b + 1) * set_count, :]
            carry = rho * carry + weight_ref[b] * one
            quad = quad + (1.0 if b == 0 else 1.0 - rho * rho) * (carry * carry)
    margin = IM_SCALE * jnp.sqrt(1.0 + quad)
    spread = jnp.tanh(set_value / VALUE_SCALE)
    eye = jnp.where(iota((NB, 128), 0) == iota((NB, 128), 1), 1.0, 0.0).astype(BF16)
    basis = dot_nt(eye, states[:, 0:128])
    at = iota(basis.shape, 0)
    basis = jnp.where(at < NF, basis, jnp.where(at == NF, 1.0, 0.0))
    sums = []
    for d in range(DATES):
        own = slice(d * paths, (d + 1) * paths)
        t, m = spread[:, own], margin[:, own]
        some = basis[:, own].astype(BF16)
        ones = jnp.where(iota(some.shape, 0) == NB - 1, 1.0, 0.0).astype(BF16)
        first, second = pieces(jnp.concatenate([t, m], axis=0), 3), pieces(jnp.concatenate([t * t, t * m], axis=0), 3)
        sums.append(sum(dot_nt(some, piece) for piece in first) + sum(dot_nt(ones, piece) for piece in second))
        value_ref[d] = set_value[:, own]
        out_ref[d * set_count : (d + 1) * set_count, :] = set_value[:, own].astype(BF16)
        base = DATES * set_count
        out_ref[base + d * NB : base + (d + 1) * NB, :] = some
    base = DATES * (set_count + NB)
    sums = pieces(jnp.concatenate(sums, axis=1), 3)
    width = 2 * DATES * set_count
    for i, piece in enumerate(sums):
        row, lane = base + i // 2 * NB, i % 2 * width
        out_ref[row : row + NB, lane : lane + width] = piece
    out_ref[base + NB : base + 2 * NB, width : 2 * width] = jnp.zeros((NB, width), BF16)


def fit_kernel(groups, set_count, value_ref, *refs):
    parts, (fit_ref, pos_ref) = refs[:groups], refs[groups:]
    paths = parts[0].shape[1]
    paths_all = groups * paths
    ridge = RIDGE * paths_all
    width = 2 * DATES * set_count
    base = DATES * (set_count + NB)
    total = sum(p[base : base + 2 * NB, :].astype(F32) for p in parts)
    total = total[0:NB, 0:width] + total[0:NB, width : 2 * width] + total[NB : 2 * NB, 0:width]
    shape = (NB, width)
    row, lane = iota(shape, 0), iota(shape, 1)
    shift = 2 * set_count
    bases, sums, works = [], [], []
    for d in range(DATES):
        first = DATES * set_count + d * NB
        basis = jnp.concatenate([p[first : first + NB, :] for p in parts], axis=1)
        blank = jnp.zeros((shift, basis.shape[1]), BF16)
        placed = jnp.concatenate([blank, basis, blank[: width - shift - NB]], axis=0)
        gram = dot_nt(basis, placed)
        gram = jnp.where(lane - shift == row, gram + ridge, gram)
        part = pltpu.roll(total, width - d * shift, 1) if d else total
        bases.append(basis)
        sums.append(part)
        works.append(jnp.where(lane < shift, jnp.where(row < NB - 1, part, 0.0), gram))
    for j in range(NB - 1):
        for d in range(DATES):
            work = works[d]
            col = jnp.broadcast_to(work[:, shift + j : shift + j + 1], shape)
            inv = 1.0 / jnp.broadcast_to(col[j : j + 1, :], shape)
            pivot = jnp.broadcast_to(work[j : j + 1, :], shape) * inv
            works[d] = jnp.where(row == j, pivot, work - col * pivot)
    flats = []
    for d in range(DATES):
        part, basis = sums[d], bases[d]
        right = jnp.where(row < NB - 1, works[d], 0.0)
        solved = pltpu.roll(right, width - set_count, 1)
        square = part[NB - 1 : NB] + ridge
        cross = pltpu.roll(part[NB - 1 : NB], width - set_count, 1)
        here = iota((1, width), 1) < set_count
        below = jnp.where(here, square - jnp.sum(part * right, axis=0, keepdims=True), 1.0)
        above = cross - jnp.sum(part * solved, axis=0, keepdims=True)
        slope = jnp.where(here, above / below, 0.0)
        coef = jnp.where(row < NB - 1, solved - right * slope, slope)
        coef = jnp.concatenate([coef, jnp.zeros((width - NB, width), F32)], axis=0).T
        coef = coef[0:set_count]
        values = [value_ref[d]] + [p[d * set_count : (d + 1) * set_count, :].astype(F32) for p in parts[1:]]
        values = jnp.concatenate(values, axis=1)
        linear = sum(dot(piece[:, 0:NB], basis) for piece in pieces(coef, 3))
        fitted = linear + coef[:, NB - 1 : NB] * jnp.tanh(values * (1.0 / VALUE_SCALE))
        fit_ref[d] = fitted[:, 0:paths]
        positive = jnp.sum(jnp.maximum(values - fitted, 0.0), axis=1, keepdims=True)
        flats.append(jnp.broadcast_to(positive * (1.0 / paths_all), (set_count, 128)))
    flats.append(jnp.zeros((128 - DATES * set_count, 128), F32))
    flat = jnp.concatenate(flats, axis=0).T
    for d in range(DATES):
        moved = pltpu.roll(flat, 128 - d * set_count, 1) if d else flat
        pos_ref[d : d + 1, :] = moved[0:1, 0:set_count]


def smem():
    return pl.BlockSpec(memory_space=pltpu.SMEM)


def vmem(count):
    return [pl.BlockSpec(memory_space=pltpu.VMEM)] * count


def params():
    return pltpu.CompilerParams(vmem_limit_bytes=VMEM_LIMIT)


def turn(x, axis, k):
    n = lax.axis_size(axis)
    return lax.ppermute(x, axis, [(i, (i + k) % n) for i in range(n)])


def meet(x, axis, k):
    n = lax.axis_size(axis)
    return lax.ppermute(x, axis, [(i, i ^ k) for i in range(n)])


def on_device(
    path_states, trade_loads, trade_amounts, trade_legs, trade_set, set_slot, risk_weights
):
    owners = lax.axis_size("trades")
    groups = lax.axis_size("paths")
    trades, factors = trade_loads.shape
    sets = set_slot.shape[0]
    set_count = sets // owners
    cap = 5 * trades // (2 * owners)
    paths = path_states.shape[1]
    cols = DATES * paths
    count = owners * cap
    block = (cap + META, factors)
    few = owners <= 8
    me = lax.axis_index("trades").astype(jnp.int32)
    if few:
        shape = [jax.ShapeDtypeStruct(block, BF16)] * owners
    else:
        me = jnp.zeros_like(me)
        shape = [jax.ShapeDtypeStruct((owners,) + block, BF16)]
    packed = pl.pallas_call(
        lambda *refs: pack_kernel(owners, cap, set_count, *refs),
        out_shape=shape,
        in_specs=[smem()] + vmem(5),
        out_specs=vmem(len(shape)),
        compiler_params=params(),
        name="pack",
    )(
        me.reshape(1),
        trade_set.reshape(1, trades),
        set_slot.reshape(1, sets),
        trade_amounts,
        trade_legs,
        trade_loads,
    )
    states = path_states.reshape(cols, factors)
    reduced = jax.ShapeDtypeStruct(((B + 1) * set_count, cols), F32)

    def scratch(batch):
        rows = batch * cap
        wide = -(-rows // 128) * 128
        return [
            pltpu.VMEM((rows, cols), F32),
            pltpu.VMEM((2 * wide, cols), BF16),
            pltpu.VMEM((wide, cols), BF16),
            pltpu.VMEM((wide, cols), BF16),
            pltpu.VMEM((B * set_count, 2 * wide), BF16),
        ]

    at, sofar, fetched = 0, [], []
    if few:
        got = [packed[0]] + [meet(packed[k], "trades", k) for k in range(1, owners)]
        if owners > EARLY:
            at = EARLY
            sofar = pl.pallas_call(
                lambda *refs: add_kernel(cap, set_count, *refs),
                out_shape=[reduced],
                in_specs=vmem(1 + at),
                out_specs=vmem(1),
                scratch_shapes=scratch(at),
                compiler_params=params(),
                name="add",
            )(states, *got[:at])
            fetched = [pltpu.VMEM(reduced.shape, F32), pltpu.SemaphoreType.DMA(())]
        last, held = got[at:], owners - at
    else:
        last, held = [lax.all_to_all(packed[0], "trades", split_axis=0, concat_axis=0, tiled=True)], owners
    packet = (DATES * (set_count + NB) + 2 * NB, paths)
    mine, value = pl.pallas_call(
        lambda *refs: owner_kernel(owners, at, cap, set_count, *refs),
        out_shape=[
            jax.ShapeDtypeStruct(packet, BF16),
            jax.ShapeDtypeStruct((DATES, set_count, paths), F32),
        ],
        in_specs=[smem()] + vmem(1) + [pl.BlockSpec(memory_space=pl.ANY)] * len(sofar) + vmem(len(last)),
        out_specs=vmem(2),
        scratch_shapes=fetched + scratch(held),
        compiler_params=params(),
        name="owner",
    )(risk_weights, states, *sofar, *last)
    parts = [mine] + [turn(mine, "paths", k) for k in range(1, groups)]
    fitted_margin, exposure = pl.pallas_call(
        lambda *refs: fit_kernel(groups, set_count, *refs),
        out_shape=[
            jax.ShapeDtypeStruct((DATES, set_count, paths), F32),
            jax.ShapeDtypeStruct((DATES, set_count), F32),
        ],
        in_specs=vmem(1 + groups),
        out_specs=vmem(2),
        compiler_params=params(),
        name="fit",
    )(value, *parts)
    return (fitted_margin, exposure)


def solution(mesh):
    in_specs = (
        P(None, "paths", None),
        P("trades", None),
        P(None, "trades"),
        P(None, "trades"),
        P("trades"),
        P(),
        P(),
    )
    out_specs = (P(None, "trades", "paths"), P(None, "trades"))
    return jax.shard_map(
        on_device, mesh=mesh, in_specs=in_specs, out_specs=out_specs, check_vma=False
    )
```

```python
import math

import jax
import jax.numpy as jnp
from jax import lax
from jax.experimental import pallas as pl
from jax.experimental.pallas import tpu as pltpu
from jax.sharding import PartitionSpec as P

B = 40
NB = 16
DATES = 2
NF = NB - 2
META = 8
EARLY = 5
STEP = 8
HALF = 256

CORR_LEN = 8.0
IM_SCALE = 0.2
RIDGE = 0.05
VALUE_SCALE = 4.0

F32 = jnp.float32
BF16 = jnp.bfloat16
VMEM_LIMIT = 40 << 20
NT = (((1,), (1,)), ((), ()))


def iota(shape, axis):
    return lax.broadcasted_iota(jnp.int32, shape, axis)


def dot(a, b):
    return jnp.dot(a, b, preferred_element_type=F32)


def dot_nt(a, b):
    return lax.dot_general(a, b, NT, preferred_element_type=F32)


def pieces(x, count):
    out = []
    for _ in range(count):
        piece = x.astype(BF16)
        out.append(piece)
        x = x - piece.astype(F32)
    return out


def pick_rows(rows, height):
    width = rows[0].shape[1]
    at = iota((height, width), 0)
    out = jnp.zeros((height, width), F32)
    for i, row in enumerate(rows):
        out = jnp.where(at == i, row, out)
    return out


def pack_kernel(owners, cap, set_count, me_ref, *refs):
    outs, held, arrived = refs[5:-6], refs[-6:-1], refs[-1]
    copies = [pltpu.make_async_copy(refs[i], held[i], arrived.at[i]) for i in range(5)]
    for copy in copies:
        copy.start()
    set_ref, slot_ref, amount_ref, leg_ref, load_ref = held
    for copy in copies[:4]:
        copy.wait()
    trades = set_ref.shape[1]
    sets = slot_ref.shape[1]
    slot = slot_ref[...].astype(F32)
    slot_owner = jnp.floor((slot + 0.5) * (1.0 / set_count))
    slot_local = slot - slot_owner * set_count
    digits = pick_rows([slot_owner, slot_local], 16).astype(BF16)
    member = jnp.where(iota((sets, trades), 0) == set_ref[...], 1.0, 0.0).astype(BF16)
    found = dot(digits, member)
    owner, local = found[0:1], found[1:2]
    height = -(-owners // 16) * 16
    marks = jnp.where(iota((height, trades), 0).astype(F32) == owner, 1.0, 0.0)
    ahead = jnp.where(iota((trades, trades), 0) < iota((trades, trades), 1), 1.0, 0.0).astype(BF16)
    rank = jnp.sum(dot(marks.astype(BF16), ahead) * marks, axis=0, keepdims=True)
    target = (owner * cap + rank).astype(jnp.int32)
    amounts = amount_ref[...]
    legs = leg_ref[...].astype(F32)
    meta = [p.astype(F32) for p in pieces(amounts[0:1], 3) + pieces(amounts[1:2], 3)]
    meta = pick_rows(meta + [legs[0:1], legs[1:2], local], 16).astype(BF16)
    copies[4].wait()
    group = 8 if owners > 8 else owners
    for base in range(0, owners, group):
        chosen, places = range(base, base + group), []
        for k in chosen:
            spot = target - (me_ref[0] ^ k) * cap
            spot = jnp.where((spot >= 0) & (spot < cap), spot + (k * cap) % 128, -1)
            places.append(jnp.where(iota((HALF, trades), 0) == spot, 1.0, 0.0).astype(BF16))
        aligned = (group * cap) % 128 == 0 and cap % 16 == 0
        if aligned:
            rows = [p[(k * cap) % 128 : (k * cap) % 128 + cap] for k, p in zip(chosen, places)]
            moved = dot(jnp.concatenate(rows, axis=0), load_ref[...])
        for i, k in enumerate(chosen):
            tags = dot_nt(meta, places[i]).astype(BF16)
            out = outs[k] if len(outs) > 1 else outs[0].at[k]
            if aligned:
                out[0:cap, :] = moved[i * cap : (i + 1) * cap].astype(BF16)
            else:
                whole = dot(places[i], load_ref[...])
                out[0:cap, :] = whole[(k * cap) % 128 : (k * cap) % 128 + cap].astype(BF16)
            out[cap : cap + META, 0:HALF] = tags[0:META]
            out[cap : cap + META, HALF : 2 * HALF] = tags[META : 2 * META]


def side_by_side(blocks, at, cap, width):
    start = at * cap // 128 * 128
    tiles = [None] * (width // 128 + 2)
    for i, block in enumerate(blocks):
        first = ((at + i) * cap - start) // 128
        for j in range(HALF // 128):
            low = block[cap : cap + META, j * 128 : (j + 1) * 128]
            high = block[cap : cap + META, HALF + j * 128 : HALF + (j + 1) * 128]
            tile = jnp.concatenate([low, high], axis=0).astype(F32)
            tiles[first + j] = tile if tiles[first + j] is None else tiles[first + j] + tile
    tiles = [jnp.zeros((2 * META, 128), F32) if t is None else t for t in tiles]
    shift = at * cap - start
    if not shift:
        return jnp.concatenate(tiles[: width // 128], axis=1)
    meta = jnp.concatenate(tiles, axis=1)
    return pltpu.roll(meta, meta.shape[1] - shift, 1)[:, :width]


def price(blocks, at, cap, set_count, states, scratch):
    level_ref, terms_ref, high_ref, low_ref, place_ref = scratch
    count = len(blocks) * cap
    width = high_ref.shape[0]
    loads = jnp.concatenate([block[0:cap, :] for block in blocks], axis=0)
    level_ref[...] = dot_nt(loads, states)
    meta = side_by_side(blocks, at, cap, width)
    eye = jnp.where(iota((16, 128), 0) % 2 == iota((16, 128), 1), 1.0, 0.0).astype(BF16)
    turned = pick_rows([meta[i : i + 1] for i in (0, 3, 1, 4, 2, 5)], 16).astype(BF16)
    columns = lax.dot_general(turned, eye, (((0,), (0,)), ((), ())), preferred_element_type=F32)
    step = math.gcd(count, 128)
    for r in range(0, count, step):
        x = level_ref[r : r + step, :]
        a = columns[r : r + step, 0:1]
        c = columns[r : r + step, 1:2]
        e = jnp.exp(-jnp.abs(x))
        more = 1.0 + e
        tail = jnp.log(more)
        near = 1.0 / more
        far = e * near
        up = x >= 0.0
        value = a * (jnp.maximum(x, 0.0) + tail) + c * (jnp.maximum(-x, 0.0) + tail)
        terms_ref[r : r + step, :] = (a * jnp.where(up, near, far)).astype(BF16)
        terms_ref[width + r : width + r + step, :] = (-c * jnp.where(up, far, near)).astype(BF16)
        high = value.astype(BF16)
        high_ref[r : r + step, :] = high
        low_ref[r : r + step, :] = (value - high.astype(F32)).astype(BF16)
    if width > count:
        for ref, first in ((terms_ref, 0), (terms_ref, width), (high_ref, 0), (low_ref, 0)):
            ref[first + count : first + width, :] = jnp.zeros((width - count, ref.shape[1]), BF16)
    in_set = jnp.where(iota((set_count, width), 0).astype(F32) == meta[8:9], 1.0, 0.0)

    def bucket_deltas(first, last):
        rows = slice(first * set_count, last * set_count)
        for leg in range(2):
            for b in range(first, last):
                place_ref[b * set_count : (b + 1) * set_count, leg * width : (leg + 1) * width] = (
                    jnp.where(meta[6 + leg : 7 + leg] == float(b), in_set, 0.0).astype(BF16)
                )
        return dot(place_ref[rows, :], terms_ref[...])

    named = in_set.astype(BF16)
    return bucket_deltas, dot(named, high_ref[...]) + dot(named, low_ref[...])


def add_kernel(cap, set_count, state_ref, *refs):
    scratch, out_ref, blocks = refs[-5:], refs[-6], refs[:-6]
    deltas, value = price(blocks, 0, cap, set_count, state_ref[...], scratch)
    for b in range(0, B, STEP):
        out_ref[b * set_count : (b + STEP) * set_count, :] = deltas(b, b + STEP)
    out_ref[B * set_count :, :] = value


def owner_kernel(owners, at, cap, set_count, weight_ref, state_ref, *refs):
    out_ref, value_ref = refs[-7:-5]
    blocks = refs[1:-7] if at else refs[:-7]
    sofar_ref = refs[0]
    if len(blocks) == 1 and owners > 1:
        blocks = [blocks[0].at[k] for k in range(owners)]
    cols = state_ref.shape[0]
    paths = cols // DATES
    states = state_ref[...]
    deltas, set_value = price(blocks, at, cap, set_count, states, refs[-5:])
    if at:
        set_value = set_value + sofar_ref[B * set_count :, :]
    rho = math.exp(-1.0 / CORR_LEN)
    carry = jnp.zeros((set_count, cols), F32)
    quad = jnp.zeros((set_count, cols), F32)
    for first in range(B - STEP, -1, -STEP):
        delta = deltas(first, first + STEP)
        for b in range(first + STEP - 1, first - 1, -1):
            one = delta[(b - first) * set_count : (b - first + 1) * set_count]
            if at:
                one = one + sofar_ref[b * set_count : (b + 1) * set_count, :]
            carry = rho * carry + weight_ref[b] * one
            quad = quad + (1.0 if b == 0 else 1.0 - rho * rho) * (carry * carry)
    margin = IM_SCALE * jnp.sqrt(1.0 + quad)
    spread = jnp.tanh(set_value / VALUE_SCALE)
    eye = jnp.where(iota((NB, 128), 0) == iota((NB, 128), 1), 1.0, 0.0).astype(BF16)
    basis = dot_nt(eye, states[:, 0:128])
    at = iota(basis.shape, 0)
    basis = jnp.where(at < NF, basis, jnp.where(at == NF, 1.0, 0.0))
    sums = []
    for d in range(DATES):
        own = slice(d * paths, (d + 1) * paths)
        t, m = spread[:, own], margin[:, own]
        some = basis[:, own].astype(BF16)
        ones = jnp.where(iota(some.shape, 0) == NB - 1, 1.0, 0.0).astype(BF16)
        first, second = pieces(jnp.concatenate([t, m], axis=0), 3), pieces(jnp.concatenate([t * t, t * m], axis=0), 3)
        sums.append(sum(dot_nt(some, piece) for piece in first) + sum(dot_nt(ones, piece) for piece in second))
        value_ref[d] = set_value[:, own]
        out_ref[d * set_count : (d + 1) * set_count, :] = set_value[:, own].astype(BF16)
        base = DATES * set_count
        out_ref[base + d * NB : base + (d + 1) * NB, :] = some
    base = DATES * (set_count + NB)
    sums = pieces(jnp.concatenate(sums, axis=1), 3)
    width = 2 * DATES * set_count
    for i, piece in enumerate(sums):
        row, lane = base + i // 2 * NB, i % 2 * width
        out_ref[row : row + NB, lane : lane + width] = piece
    out_ref[base + NB : base + 2 * NB, width : 2 * width] = jnp.zeros((NB, width), BF16)


def fit_kernel(groups, set_count, value_ref, *refs):
    parts, (fit_ref, pos_ref) = refs[:groups], refs[groups:]
    paths = parts[0].shape[1]
    paths_all = groups * paths
    ridge = RIDGE * paths_all
    width = 2 * DATES * set_count
    base = DATES * (set_count + NB)
    total = sum(p[base : base + 2 * NB, :].astype(F32) for p in parts)
    total = total[0:NB, 0:width] + total[0:NB, width : 2 * width] + total[NB : 2 * NB, 0:width]
    shape = (NB, width)
    row, lane = iota(shape, 0), iota(shape, 1)
    shift = 2 * set_count
    bases, sums, works = [], [], []
    for d in range(DATES):
        first = DATES * set_count + d * NB
        basis = jnp.concatenate([p[first : first + NB, :] for p in parts], axis=1)
        blank = jnp.zeros((shift, basis.shape[1]), BF16)
        placed = jnp.concatenate([blank, basis, blank[: width - shift - NB]], axis=0)
        gram = dot_nt(basis, placed)
        gram = jnp.where(lane - shift == row, gram + ridge, gram)
        part = pltpu.roll(total, width - d * shift, 1) if d else total
        bases.append(basis)
        sums.append(part)
        works.append(jnp.where(lane < shift, jnp.where(row < NB - 1, part, 0.0), gram))
    for j in range(NB - 1):
        for d in range(DATES):
            work = works[d]
            col = jnp.broadcast_to(work[:, shift + j : shift + j + 1], shape)
            inv = 1.0 / jnp.broadcast_to(col[j : j + 1, :], shape)
            pivot = jnp.broadcast_to(work[j : j + 1, :], shape) * inv
            works[d] = jnp.where(row == j, pivot, work - col * pivot)
    flats = []
    for d in range(DATES):
        part, basis = sums[d], bases[d]
        right = jnp.where(row < NB - 1, works[d], 0.0)
        solved = pltpu.roll(right, width - set_count, 1)
        square = part[NB - 1 : NB] + ridge
        cross = pltpu.roll(part[NB - 1 : NB], width - set_count, 1)
        here = iota((1, width), 1) < set_count
        below = jnp.where(here, square - jnp.sum(part * right, axis=0, keepdims=True), 1.0)
        above = cross - jnp.sum(part * solved, axis=0, keepdims=True)
        slope = jnp.where(here, above / below, 0.0)
        coef = jnp.where(row < NB - 1, solved - right * slope, slope)
        coef = jnp.concatenate([coef, jnp.zeros((width - NB, width), F32)], axis=0).T
        coef = coef[0:set_count]
        values = [value_ref[d]] + [p[d * set_count : (d + 1) * set_count, :].astype(F32) for p in parts[1:]]
        values = jnp.concatenate(values, axis=1)
        linear = sum(dot(piece[:, 0:NB], basis) for piece in pieces(coef, 3))
        fitted = linear + coef[:, NB - 1 : NB] * jnp.tanh(values * (1.0 / VALUE_SCALE))
        fit_ref[d] = fitted[:, 0:paths]
        positive = jnp.sum(jnp.maximum(values - fitted, 0.0), axis=1, keepdims=True)
        flats.append(jnp.broadcast_to(positive * (1.0 / paths_all), (set_count, 128)))
    flats.append(jnp.zeros((128 - DATES * set_count, 128), F32))
    flat = jnp.concatenate(flats, axis=0).T
    for d in range(DATES):
        moved = pltpu.roll(flat, 128 - d * set_count, 1) if d else flat
        pos_ref[d : d + 1, :] = moved[0:1, 0:set_count]


def smem():
    return pl.BlockSpec(memory_space=pltpu.SMEM)


def vmem(count):
    return [pl.BlockSpec(memory_space=pltpu.VMEM)] * count


def params():
    return pltpu.CompilerParams(vmem_limit_bytes=VMEM_LIMIT)


def near(x):
    return pltpu.with_memory_space_constraint(x, pltpu.VMEM)


def turn(x, axis, k):
    n = lax.axis_size(axis)
    return near(lax.ppermute(x, axis, [(i, (i + k) % n) for i in range(n)]))


def meet(x, axis, k):
    n = lax.axis_size(axis)
    return near(lax.ppermute(x, axis, [(i, i ^ k) for i in range(n)]))


def on_device(
    path_states, trade_loads, trade_amounts, trade_legs, trade_set, set_slot, risk_weights
):
    owners = lax.axis_size("trades")
    groups = lax.axis_size("paths")
    trades, factors = trade_loads.shape
    sets = set_slot.shape[0]
    set_count = sets // owners
    cap = 5 * trades // (2 * owners)
    paths = path_states.shape[1]
    cols = DATES * paths
    count = owners * cap
    block = (cap + META, factors)
    few = owners <= 8
    me = lax.axis_index("trades").astype(jnp.int32)
    if few:
        shape = [pltpu.VMEM(block, BF16)] * owners
    else:
        me = jnp.zeros_like(me)
        shape = [jax.ShapeDtypeStruct((owners,) + block, BF16)]
    inputs = (
        trade_set.reshape(1, trades),
        set_slot.reshape(1, sets),
        trade_amounts,
        trade_legs,
        trade_loads,
    )
    packed = pl.pallas_call(
        lambda *refs: pack_kernel(owners, cap, set_count, *refs),
        out_shape=shape,
        in_specs=[smem()] + [pl.BlockSpec(memory_space=pltpu.HBM)] * 5,
        out_specs=vmem(len(shape)),
        scratch_shapes=[pltpu.VMEM(x.shape, x.dtype) for x in inputs] + [pltpu.SemaphoreType.DMA((5,))],
        compiler_params=params(),
        name="pack",
    )(me.reshape(1), *[pltpu.with_memory_space_constraint(x, pltpu.HBM) for x in inputs])
    states = path_states.reshape(cols, factors)
    reduced = pltpu.VMEM(((B + 1) * set_count, cols), F32)

    def scratch(batch):
        rows = batch * cap
        wide = -(-rows // 128) * 128
        return [
            pltpu.VMEM((rows, cols), F32),
            pltpu.VMEM((2 * wide, cols), BF16),
            pltpu.VMEM((wide, cols), BF16),
            pltpu.VMEM((wide, cols), BF16),
            pltpu.VMEM((B * set_count, 2 * wide), BF16),
        ]

    at, sofar = 0, []
    if few:
        got = [near(packed[0])] + [meet(packed[k], "trades", k) for k in range(1, owners)]
        if owners > EARLY:
            at = EARLY
            sofar = pl.pallas_call(
                lambda *refs: add_kernel(cap, set_count, *refs),
                out_shape=[reduced],
                in_specs=vmem(1 + at),
                out_specs=vmem(1),
                scratch_shapes=scratch(at),
                compiler_params=params(),
                name="add",
            )(states, *got[:at])
            sofar = [near(sofar[0])]
        last, held = got[at:], owners - at
    else:
        last, held = [lax.all_to_all(packed[0], "trades", split_axis=0, concat_axis=0, tiled=True)], owners
    packet = (DATES * (set_count + NB) + 2 * NB, paths)
    mine, value = pl.pallas_call(
        lambda *refs: owner_kernel(owners, at, cap, set_count, *refs),
        out_shape=[
            pltpu.VMEM(packet, BF16),
            pltpu.VMEM((DATES, set_count, paths), F32),
        ],
        in_specs=[smem()] + vmem(1 + len(sofar) + len(last)),
        out_specs=vmem(2),
        scratch_shapes=scratch(held),
        compiler_params=params(),
        name="owner",
    )(risk_weights, states, *sofar, *last)
    parts = [near(mine)] + [turn(mine, "paths", k) for k in range(1, groups)]
    fitted_margin, exposure = pl.pallas_call(
        lambda *refs: fit_kernel(groups, set_count, *refs),
        out_shape=[
            jax.ShapeDtypeStruct((DATES, set_count, paths), F32),
            jax.ShapeDtypeStruct((DATES, set_count), F32),
        ],
        in_specs=vmem(1 + groups),
        out_specs=vmem(2),
        compiler_params=params(),
        name="fit",
    )(near(value), *parts)
    return (fitted_margin, exposure)


def solution(mesh):
    in_specs = (
        P(None, "paths", None),
        P("trades", None),
        P(None, "trades"),
        P(None, "trades"),
        P("trades"),
        P(),
        P(),
    )
    out_specs = (P(None, "trades", "paths"), P(None, "trades"))
    return jax.shard_map(
        on_device, mesh=mesh, in_specs=in_specs, out_specs=out_specs, check_vma=False
    )
```

```python
import math

import jax
import jax.numpy as jnp
from jax import lax
from jax.experimental import pallas as pl
from jax.experimental.pallas import tpu as pltpu
from jax.sharding import PartitionSpec as P

B = 40
NB = 16
DATES = 2
NF = NB - 2
META = 8
EARLY = 5
ORDER = (0, 2, 4, 3, 1, 5, 6, 7)
STEP = 8
HALF = 256

CORR_LEN = 8.0
IM_SCALE = 0.2
RIDGE = 0.05
VALUE_SCALE = 4.0

F32 = jnp.float32
BF16 = jnp.bfloat16
VMEM_LIMIT = 40 << 20
NT = (((1,), (1,)), ((), ()))


def iota(shape, axis):
    return lax.broadcasted_iota(jnp.int32, shape, axis)


def dot(a, b):
    return jnp.dot(a, b, preferred_element_type=F32)


def dot_nt(a, b):
    return lax.dot_general(a, b, NT, preferred_element_type=F32)


def pieces(x, count):
    out = []
    for _ in range(count):
        piece = x.astype(BF16)
        out.append(piece)
        x = x - piece.astype(F32)
    return out


def pick_rows(rows, height):
    width = rows[0].shape[1]
    at = iota((height, width), 0)
    out = jnp.zeros((height, width), F32)
    for i, row in enumerate(rows):
        out = jnp.where(at == i, row, out)
    return out


def pack_kernel(owners, order, cap, set_count, me_ref, *refs):
    outs, held, arrived = refs[5:-6], refs[-6:-1], refs[-1]
    copies = [pltpu.make_async_copy(refs[i], held[i], arrived.at[i]) for i in range(5)]
    for copy in copies:
        copy.start()
    set_ref, slot_ref, amount_ref, leg_ref, load_ref = held
    for copy in copies[:4]:
        copy.wait()
    trades = set_ref.shape[1]
    sets = slot_ref.shape[1]
    slot = slot_ref[...].astype(F32)
    slot_owner = jnp.floor((slot + 0.5) * (1.0 / set_count))
    slot_local = slot - slot_owner * set_count
    digits = pick_rows([slot_owner, slot_local], 16).astype(BF16)
    member = jnp.where(iota((sets, trades), 0) == set_ref[...], 1.0, 0.0).astype(BF16)
    found = dot(digits, member)
    owner, local = found[0:1], found[1:2]
    height = -(-owners // 16) * 16
    marks = jnp.where(iota((height, trades), 0).astype(F32) == owner, 1.0, 0.0)
    ahead = jnp.where(iota((trades, trades), 0) < iota((trades, trades), 1), 1.0, 0.0).astype(BF16)
    rank = jnp.sum(dot(marks.astype(BF16), ahead) * marks, axis=0, keepdims=True)
    target = (owner * cap + rank).astype(jnp.int32)
    amounts = amount_ref[...]
    legs = leg_ref[...].astype(F32)
    meta = [p.astype(F32) for p in pieces(amounts[0:1], 3) + pieces(amounts[1:2], 3)]
    meta = pick_rows(meta + [legs[0:1], legs[1:2], local], 16).astype(BF16)
    copies[4].wait()
    group = 8 if owners > 8 else owners
    for base in range(0, owners, group):
        chosen, places = range(base, base + group), []
        for k in chosen:
            spot = target - (me_ref[0] ^ order[k]) * cap
            spot = jnp.where((spot >= 0) & (spot < cap), spot + (k * cap) % 128, -1)
            places.append(jnp.where(iota((HALF, trades), 0) == spot, 1.0, 0.0).astype(BF16))
        aligned = (group * cap) % 128 == 0 and cap % 16 == 0
        if aligned:
            rows = [p[(k * cap) % 128 : (k * cap) % 128 + cap] for k, p in zip(chosen, places)]
            moved = dot(jnp.concatenate(rows, axis=0), load_ref[...])
        for i, k in enumerate(chosen):
            tags = dot_nt(meta, places[i]).astype(BF16)
            out = outs[k] if len(outs) > 1 else outs[0].at[k]
            if aligned:
                out[0:cap, :] = moved[i * cap : (i + 1) * cap].astype(BF16)
            else:
                whole = dot(places[i], load_ref[...])
                out[0:cap, :] = whole[(k * cap) % 128 : (k * cap) % 128 + cap].astype(BF16)
            out[cap : cap + META, 0:HALF] = tags[0:META]
            out[cap : cap + META, HALF : 2 * HALF] = tags[META : 2 * META]


def side_by_side(blocks, at, cap, width):
    start = at * cap // 128 * 128
    tiles = [None] * (width // 128 + 2)
    for i, block in enumerate(blocks):
        first = ((at + i) * cap - start) // 128
        for j in range(HALF // 128):
            low = block[cap : cap + META, j * 128 : (j + 1) * 128]
            high = block[cap : cap + META, HALF + j * 128 : HALF + (j + 1) * 128]
            tile = jnp.concatenate([low, high], axis=0).astype(F32)
            tiles[first + j] = tile if tiles[first + j] is None else tiles[first + j] + tile
    tiles = [jnp.zeros((2 * META, 128), F32) if t is None else t for t in tiles]
    shift = at * cap - start
    if not shift:
        return jnp.concatenate(tiles[: width // 128], axis=1)
    meta = jnp.concatenate(tiles, axis=1)
    return pltpu.roll(meta, meta.shape[1] - shift, 1)[:, :width]


def price(blocks, at, cap, set_count, states, scratch):
    level_ref, terms_ref, high_ref, low_ref, place_ref = scratch
    count = len(blocks) * cap
    width = high_ref.shape[0]
    loads = jnp.concatenate([block[0:cap, :] for block in blocks], axis=0)
    level_ref[...] = dot_nt(loads, states)
    meta = side_by_side(blocks, at, cap, width)
    eye = jnp.where(iota((16, 128), 0) % 2 == iota((16, 128), 1), 1.0, 0.0).astype(BF16)
    turned = pick_rows([meta[i : i + 1] for i in (0, 3, 1, 4, 2, 5)], 16).astype(BF16)
    columns = lax.dot_general(turned, eye, (((0,), (0,)), ((), ())), preferred_element_type=F32)
    step = math.gcd(count, 128)
    for r in range(0, count, step):
        x = level_ref[r : r + step, :]
        a = columns[r : r + step, 0:1]
        c = columns[r : r + step, 1:2]
        e = jnp.exp(-jnp.abs(x))
        more = 1.0 + e
        tail = jnp.log(more)
        near = 1.0 / more
        far = e * near
        up = x >= 0.0
        value = a * (jnp.maximum(x, 0.0) + tail) + c * (jnp.maximum(-x, 0.0) + tail)
        terms_ref[r : r + step, :] = (a * jnp.where(up, near, far)).astype(BF16)
        terms_ref[width + r : width + r + step, :] = (-c * jnp.where(up, far, near)).astype(BF16)
        high = value.astype(BF16)
        high_ref[r : r + step, :] = high
        low_ref[r : r + step, :] = (value - high.astype(F32)).astype(BF16)
    if width > count:
        for ref, first in ((terms_ref, 0), (terms_ref, width), (high_ref, 0), (low_ref, 0)):
            ref[first + count : first + width, :] = jnp.zeros((width - count, ref.shape[1]), BF16)
    in_set = jnp.where(iota((set_count, width), 0).astype(F32) == meta[8:9], 1.0, 0.0)

    def bucket_deltas(first, last):
        rows = slice(first * set_count, last * set_count)
        for leg in range(2):
            for b in range(first, last):
                place_ref[b * set_count : (b + 1) * set_count, leg * width : (leg + 1) * width] = (
                    jnp.where(meta[6 + leg : 7 + leg] == float(b), in_set, 0.0).astype(BF16)
                )
        return dot(place_ref[rows, :], terms_ref[...])

    named = in_set.astype(BF16)
    return bucket_deltas, dot(named, high_ref[...]) + dot(named, low_ref[...])


def add_kernel(cap, set_count, state_ref, *refs):
    scratch, out_ref, blocks = refs[-5:], refs[-6], refs[:-6]
    deltas, value = price(blocks, 0, cap, set_count, state_ref[...], scratch)
    for b in range(0, B, STEP):
        out_ref[b * set_count : (b + STEP) * set_count, :] = deltas(b, b + STEP)
    out_ref[B * set_count :, :] = value


def owner_kernel(owners, at, cap, set_count, weight_ref, state_ref, *refs):
    out_ref, value_ref = refs[-7:-5]
    blocks = refs[1:-7] if at else refs[:-7]
    sofar_ref = refs[0]
    if len(blocks) == 1 and owners > 1:
        blocks = [blocks[0].at[k] for k in range(owners)]
    cols = state_ref.shape[0]
    paths = cols // DATES
    states = state_ref[...]
    deltas, set_value = price(blocks, at, cap, set_count, states, refs[-5:])
    if at:
        set_value = set_value + sofar_ref[B * set_count :, :]
    rho = math.exp(-1.0 / CORR_LEN)
    carry = jnp.zeros((set_count, cols), F32)
    quad = jnp.zeros((set_count, cols), F32)
    for first in range(B - STEP, -1, -STEP):
        delta = deltas(first, first + STEP)
        for b in range(first + STEP - 1, first - 1, -1):
            one = delta[(b - first) * set_count : (b - first + 1) * set_count]
            if at:
                one = one + sofar_ref[b * set_count : (b + 1) * set_count, :]
            carry = rho * carry + weight_ref[b] * one
            quad = quad + (1.0 if b == 0 else 1.0 - rho * rho) * (carry * carry)
    margin = IM_SCALE * jnp.sqrt(1.0 + quad)
    spread = jnp.tanh(set_value / VALUE_SCALE)
    eye = jnp.where(iota((NB, 128), 0) == iota((NB, 128), 1), 1.0, 0.0).astype(BF16)
    basis = dot_nt(eye, states[:, 0:128])
    at = iota(basis.shape, 0)
    basis = jnp.where(at < NF, basis, jnp.where(at == NF, 1.0, 0.0))
    sums = []
    for d in range(DATES):
        own = slice(d * paths, (d + 1) * paths)
        t, m = spread[:, own], margin[:, own]
        some = basis[:, own].astype(BF16)
        ones = jnp.where(iota(some.shape, 0) == NB - 1, 1.0, 0.0).astype(BF16)
        first, second = pieces(jnp.concatenate([t, m], axis=0), 3), pieces(jnp.concatenate([t * t, t * m], axis=0), 3)
        sums.append(sum(dot_nt(some, piece) for piece in first) + sum(dot_nt(ones, piece) for piece in second))
        value_ref[d] = set_value[:, own]
        out_ref[d * set_count : (d + 1) * set_count, :] = set_value[:, own].astype(BF16)
        base = DATES * set_count
        out_ref[base + d * NB : base + (d + 1) * NB, :] = some
    base = DATES * (set_count + NB)
    sums = pieces(jnp.concatenate(sums, axis=1), 3)
    width = 2 * DATES * set_count
    for i, piece in enumerate(sums):
        row, lane = base + i // 2 * NB, i % 2 * width
        out_ref[row : row + NB, lane : lane + width] = piece
    out_ref[base + NB : base + 2 * NB, width : 2 * width] = jnp.zeros((NB, width), BF16)


def fit_kernel(groups, set_count, value_ref, *refs):
    parts, (fit_ref, pos_ref) = refs[:groups], refs[groups:]
    paths = parts[0].shape[1]
    paths_all = groups * paths
    ridge = RIDGE * paths_all
    width = 2 * DATES * set_count
    base = DATES * (set_count + NB)
    total = sum(p[base : base + 2 * NB, :].astype(F32) for p in parts)
    total = total[0:NB, 0:width] + total[0:NB, width : 2 * width] + total[NB : 2 * NB, 0:width]
    shape = (NB, width)
    row, lane = iota(shape, 0), iota(shape, 1)
    shift = 2 * set_count
    bases, sums, works = [], [], []
    for d in range(DATES):
        first = DATES * set_count + d * NB
        basis = jnp.concatenate([p[first : first + NB, :] for p in parts], axis=1)
        blank = jnp.zeros((shift, basis.shape[1]), BF16)
        placed = jnp.concatenate([blank, basis, blank[: width - shift - NB]], axis=0)
        gram = dot_nt(basis, placed)
        gram = jnp.where(lane - shift == row, gram + ridge, gram)
        part = pltpu.roll(total, width - d * shift, 1) if d else total
        bases.append(basis)
        sums.append(part)
        works.append(jnp.where(lane < shift, jnp.where(row < NB - 1, part, 0.0), gram))
    for j in range(NB - 1):
        for d in range(DATES):
            work = works[d]
            col = jnp.broadcast_to(work[:, shift + j : shift + j + 1], shape)
            inv = 1.0 / jnp.broadcast_to(col[j : j + 1, :], shape)
            pivot = jnp.broadcast_to(work[j : j + 1, :], shape) * inv
            works[d] = jnp.where(row == j, pivot, work - col * pivot)
    flats = []
    for d in range(DATES):
        part, basis = sums[d], bases[d]
        right = jnp.where(row < NB - 1, works[d], 0.0)
        solved = pltpu.roll(right, width - set_count, 1)
        square = part[NB - 1 : NB] + ridge
        cross = pltpu.roll(part[NB - 1 : NB], width - set_count, 1)
        here = iota((1, width), 1) < set_count
        below = jnp.where(here, square - jnp.sum(part * right, axis=0, keepdims=True), 1.0)
        above = cross - jnp.sum(part * solved, axis=0, keepdims=True)
        slope = jnp.where(here, above / below, 0.0)
        coef = jnp.where(row < NB - 1, solved - right * slope, slope)
        coef = jnp.concatenate([coef, jnp.zeros((width - NB, width), F32)], axis=0).T
        coef = coef[0:set_count]
        values = [value_ref[d]] + [p[d * set_count : (d + 1) * set_count, :].astype(F32) for p in parts[1:]]
        values = jnp.concatenate(values, axis=1)
        linear = sum(dot(piece[:, 0:NB], basis) for piece in pieces(coef, 3))
        fitted = linear + coef[:, NB - 1 : NB] * jnp.tanh(values * (1.0 / VALUE_SCALE))
        fit_ref[d] = fitted[:, 0:paths]
        positive = jnp.sum(jnp.maximum(values - fitted, 0.0), axis=1, keepdims=True)
        flats.append(jnp.broadcast_to(positive * (1.0 / paths_all), (set_count, 128)))
    flats.append(jnp.zeros((128 - DATES * set_count, 128), F32))
    flat = jnp.concatenate(flats, axis=0).T
    for d in range(DATES):
        moved = pltpu.roll(flat, 128 - d * set_count, 1) if d else flat
        pos_ref[d : d + 1, :] = moved[0:1, 0:set_count]


def smem():
    return pl.BlockSpec(memory_space=pltpu.SMEM)


def vmem(count):
    return [pl.BlockSpec(memory_space=pltpu.VMEM)] * count


def params():
    return pltpu.CompilerParams(vmem_limit_bytes=VMEM_LIMIT)


def near(x):
    return pltpu.with_memory_space_constraint(x, pltpu.VMEM)


def turn(x, axis, k):
    n = lax.axis_size(axis)
    return near(lax.ppermute(x, axis, [(i, (i + k) % n) for i in range(n)]))


def meet(x, axis, k):
    n = lax.axis_size(axis)
    return near(lax.ppermute(x, axis, [(i, i ^ k) for i in range(n)]))


def on_device(
    path_states, trade_loads, trade_amounts, trade_legs, trade_set, set_slot, risk_weights
):
    owners = lax.axis_size("trades")
    groups = lax.axis_size("paths")
    trades, factors = trade_loads.shape
    sets = set_slot.shape[0]
    set_count = sets // owners
    cap = 5 * trades // (2 * owners)
    paths = path_states.shape[1]
    cols = DATES * paths
    count = owners * cap
    block = (cap + META, factors)
    few = owners <= 8
    order = ORDER if owners == len(ORDER) else tuple(range(owners))
    me = lax.axis_index("trades").astype(jnp.int32)
    if few:
        shape = [pltpu.VMEM(block, BF16)] * owners
    else:
        me = jnp.zeros_like(me)
        shape = [jax.ShapeDtypeStruct((owners,) + block, BF16)]
    inputs = (
        trade_set.reshape(1, trades),
        set_slot.reshape(1, sets),
        trade_amounts,
        trade_legs,
        trade_loads,
    )
    packed = pl.pallas_call(
        lambda *refs: pack_kernel(owners, order, cap, set_count, *refs),
        out_shape=shape,
        in_specs=[smem()] + [pl.BlockSpec(memory_space=pltpu.HBM)] * 5,
        out_specs=vmem(len(shape)),
        scratch_shapes=[pltpu.VMEM(x.shape, x.dtype) for x in inputs] + [pltpu.SemaphoreType.DMA((5,))],
        compiler_params=params(),
        name="pack",
    )(me.reshape(1), *[pltpu.with_memory_space_constraint(x, pltpu.HBM) for x in inputs])
    states = path_states.reshape(cols, factors)
    reduced = pltpu.VMEM(((B + 1) * set_count, cols), F32)

    def scratch(batch):
        rows = batch * cap
        wide = -(-rows // 128) * 128
        return [
            pltpu.VMEM((rows, cols), F32),
            pltpu.VMEM((2 * wide, cols), BF16),
            pltpu.VMEM((wide, cols), BF16),
            pltpu.VMEM((wide, cols), BF16),
            pltpu.VMEM((B * set_count, 2 * wide), BF16),
        ]

    at, sofar = 0, []
    if few:
        got = [near(packed[0])] + [meet(packed[k], "trades", order[k]) for k in range(1, owners)]
        if owners > EARLY:
            at = EARLY
            sofar = pl.pallas_call(
                lambda *refs: add_kernel(cap, set_count, *refs),
                out_shape=[reduced],
                in_specs=vmem(1 + at),
                out_specs=vmem(1),
                scratch_shapes=scratch(at),
                compiler_params=params(),
                name="add",
            )(states, *got[:at])
            sofar = [near(sofar[0])]
        last, held = got[at:], owners - at
    else:
        last, held = [lax.all_to_all(packed[0], "trades", split_axis=0, concat_axis=0, tiled=True)], owners
    packet = (DATES * (set_count + NB) + 2 * NB, paths)
    mine, value = pl.pallas_call(
        lambda *refs: owner_kernel(owners, at, cap, set_count, *refs),
        out_shape=[
            pltpu.VMEM(packet, BF16),
            pltpu.VMEM((DATES, set_count, paths), F32),
        ],
        in_specs=[smem()] + vmem(1 + len(sofar) + len(last)),
        out_specs=vmem(2),
        scratch_shapes=scratch(held),
        compiler_params=params(),
        name="owner",
    )(risk_weights, states, *sofar, *last)
    parts = [near(mine)] + [meet(mine, "paths", k) for k in range(1, groups)]
    fitted_margin, exposure = pl.pallas_call(
        lambda *refs: fit_kernel(groups, set_count, *refs),
        out_shape=[
            jax.ShapeDtypeStruct((DATES, set_count, paths), F32),
            jax.ShapeDtypeStruct((DATES, set_count), F32),
        ],
        in_specs=vmem(1 + groups),
        out_specs=vmem(2),
        compiler_params=params(),
        name="fit",
    )(near(value), *parts)
    return (fitted_margin, exposure)


def solution(mesh):
    in_specs = (
        P(None, "paths", None),
        P("trades", None),
        P(None, "trades"),
        P(None, "trades"),
        P("trades"),
        P(),
        P(),
    )
    out_specs = (P(None, "trades", "paths"), P(None, "trades"))
    return jax.shard_map(
        on_device, mesh=mesh, in_specs=in_specs, out_specs=out_specs, check_vma=False
    )
```

```python
import math

import jax
import jax.numpy as jnp
from jax import lax
from jax.experimental import pallas as pl
from jax.experimental.pallas import tpu as pltpu
from jax.sharding import PartitionSpec as P

B = 40
NB = 16
DATES = 2
NF = NB - 2
META = 8
EARLY = 5
ORDER = (0, 2, 4, 3, 1, 5, 6, 7)
STEP = 4
HALF = 256

CORR_LEN = 8.0
IM_SCALE = 0.2
RIDGE = 0.05
VALUE_SCALE = 4.0

F32 = jnp.float32
BF16 = jnp.bfloat16
VMEM_LIMIT = 40 << 20
NT = (((1,), (1,)), ((), ()))


def iota(shape, axis):
    return lax.broadcasted_iota(jnp.int32, shape, axis)


def dot(a, b):
    return jnp.dot(a, b, preferred_element_type=F32)


def dot_nt(a, b):
    return lax.dot_general(a, b, NT, preferred_element_type=F32)


def pieces(x, count):
    out = []
    for _ in range(count):
        piece = x.astype(BF16)
        out.append(piece)
        x = x - piece.astype(F32)
    return out


def pick_rows(rows, height):
    width = rows[0].shape[1]
    at = iota((height, width), 0)
    out = jnp.zeros((height, width), F32)
    for i, row in enumerate(rows):
        out = jnp.where(at == i, row, out)
    return out


def pack_kernel(owners, order, cap, set_count, me_ref, *refs):
    outs, held, arrived = refs[5:-6], refs[-6:-1], refs[-1]
    copies = [pltpu.make_async_copy(refs[i], held[i], arrived.at[i]) for i in range(5)]
    for copy in copies:
        copy.start()
    set_ref, slot_ref, amount_ref, leg_ref, load_ref = held
    for copy in copies[:4]:
        copy.wait()
    trades = set_ref.shape[1]
    sets = slot_ref.shape[1]
    slot = slot_ref[...].astype(F32)
    slot_owner = jnp.floor((slot + 0.5) * (1.0 / set_count))
    slot_local = slot - slot_owner * set_count
    digits = pick_rows([slot_owner, slot_local], 16).astype(BF16)
    member = jnp.where(iota((sets, trades), 0) == set_ref[...], 1.0, 0.0).astype(BF16)
    found = dot(digits, member)
    owner, local = found[0:1], found[1:2]
    height = -(-owners // 16) * 16
    marks = jnp.where(iota((height, trades), 0).astype(F32) == owner, 1.0, 0.0)
    ahead = jnp.where(iota((trades, trades), 0) < iota((trades, trades), 1), 1.0, 0.0).astype(BF16)
    rank = jnp.sum(dot(marks.astype(BF16), ahead) * marks, axis=0, keepdims=True)
    target = (owner * cap + rank).astype(jnp.int32)
    amounts = amount_ref[...]
    legs = leg_ref[...].astype(F32)
    meta = [p.astype(F32) for p in pieces(amounts[0:1], 3) + pieces(amounts[1:2], 3)]
    meta = pick_rows(meta + [legs[0:1], legs[1:2], local], 16).astype(BF16)
    copies[4].wait()
    group = 8 if owners > 8 else owners
    for base in range(0, owners, group):
        chosen, places = range(base, base + group), []
        for k in chosen:
            spot = target - (me_ref[0] ^ order[k]) * cap
            spot = jnp.where((spot >= 0) & (spot < cap), spot + (k * cap) % 128, -1)
            places.append(jnp.where(iota((HALF, trades), 0) == spot, 1.0, 0.0).astype(BF16))
        aligned = (group * cap) % 128 == 0 and cap % 16 == 0
        if aligned:
            rows = [p[(k * cap) % 128 : (k * cap) % 128 + cap] for k, p in zip(chosen, places)]
            moved = dot(jnp.concatenate(rows, axis=0), load_ref[...])
        for i, k in enumerate(chosen):
            tags = dot_nt(meta, places[i]).astype(BF16)
            out = outs[k] if len(outs) > 1 else outs[0].at[k]
            if aligned:
                out[0:cap, :] = moved[i * cap : (i + 1) * cap].astype(BF16)
            else:
                whole = dot(places[i], load_ref[...])
                out[0:cap, :] = whole[(k * cap) % 128 : (k * cap) % 128 + cap].astype(BF16)
            out[cap : cap + META, 0:HALF] = tags[0:META]
            out[cap : cap + META, HALF : 2 * HALF] = tags[META : 2 * META]


def side_by_side(blocks, at, cap, width):
    start = at * cap // 128 * 128
    tiles = [None] * (width // 128 + 2)
    for i, block in enumerate(blocks):
        first = ((at + i) * cap - start) // 128
        for j in range(HALF // 128):
            low = block[cap : cap + META, j * 128 : (j + 1) * 128]
            high = block[cap : cap + META, HALF + j * 128 : HALF + (j + 1) * 128]
            tile = jnp.concatenate([low, high], axis=0).astype(F32)
            tiles[first + j] = tile if tiles[first + j] is None else tiles[first + j] + tile
    tiles = [jnp.zeros((2 * META, 128), F32) if t is None else t for t in tiles]
    shift = at * cap - start
    if not shift:
        return jnp.concatenate(tiles[: width // 128], axis=1)
    meta = jnp.concatenate(tiles, axis=1)
    return pltpu.roll(meta, meta.shape[1] - shift, 1)[:, :width]


def price(blocks, at, cap, set_count, states, scratch):
    level_ref, terms_ref, high_ref, low_ref, place_ref = scratch
    count = len(blocks) * cap
    width = high_ref.shape[0]
    loads = jnp.concatenate([block[0:cap, :] for block in blocks], axis=0)
    level_ref[...] = dot_nt(loads, states)
    meta = side_by_side(blocks, at, cap, width)
    eye = jnp.where(iota((16, 128), 0) % 2 == iota((16, 128), 1), 1.0, 0.0).astype(BF16)
    turned = pick_rows([meta[i : i + 1] for i in (0, 3, 1, 4, 2, 5)], 16).astype(BF16)
    columns = lax.dot_general(turned, eye, (((0,), (0,)), ((), ())), preferred_element_type=F32)
    step = math.gcd(count, 128)
    for r in range(0, count, step):
        x = level_ref[r : r + step, :]
        a = columns[r : r + step, 0:1]
        c = columns[r : r + step, 1:2]
        e = jnp.exp(-jnp.abs(x))
        more = 1.0 + e
        tail = jnp.log(more)
        near = 1.0 / more
        far = e * near
        up = x >= 0.0
        value = a * (jnp.maximum(x, 0.0) + tail) + c * (jnp.maximum(-x, 0.0) + tail)
        terms_ref[r : r + step, :] = (a * jnp.where(up, near, far)).astype(BF16)
        terms_ref[width + r : width + r + step, :] = (-c * jnp.where(up, far, near)).astype(BF16)
        high = value.astype(BF16)
        high_ref[r : r + step, :] = high
        low_ref[r : r + step, :] = (value - high.astype(F32)).astype(BF16)
    if width > count:
        for ref, first in ((terms_ref, 0), (terms_ref, width), (high_ref, 0), (low_ref, 0)):
            ref[first + count : first + width, :] = jnp.zeros((width - count, ref.shape[1]), BF16)
    in_set = jnp.where(iota((set_count, width), 0).astype(F32) == meta[8:9], 1.0, 0.0)

    def bucket_deltas(first, last):
        rows = slice(first * set_count, last * set_count)
        for leg in range(2):
            for b in range(first, last):
                place_ref[b * set_count : (b + 1) * set_count, leg * width : (leg + 1) * width] = (
                    jnp.where(meta[6 + leg : 7 + leg] == float(b), in_set, 0.0).astype(BF16)
                )
        return dot(place_ref[rows, :], terms_ref[...])

    named = in_set.astype(BF16)
    return bucket_deltas, dot(named, high_ref[...]) + dot(named, low_ref[...])


def add_kernel(cap, set_count, state_ref, *refs):
    scratch, out_ref, blocks = refs[-5:], refs[-6], refs[:-6]
    deltas, value = price(blocks, 0, cap, set_count, state_ref[...], scratch)
    for b in range(0, B, STEP):
        out_ref[b * set_count : (b + STEP) * set_count, :] = deltas(b, b + STEP)
    out_ref[B * set_count :, :] = value


def owner_kernel(owners, at, cap, set_count, weight_ref, state_ref, *refs):
    out_ref, value_ref = refs[-7:-5]
    blocks = refs[1:-7] if at else refs[:-7]
    sofar_ref = refs[0]
    if len(blocks) == 1 and owners > 1:
        blocks = [blocks[0].at[k] for k in range(owners)]
    cols = state_ref.shape[0]
    paths = cols // DATES
    states = state_ref[...]
    deltas, set_value = price(blocks, at, cap, set_count, states, refs[-5:])
    if at:
        set_value = set_value + sofar_ref[B * set_count :, :]
    rho = math.exp(-1.0 / CORR_LEN)
    carry = jnp.zeros((set_count, cols), F32)
    quad = jnp.zeros((set_count, cols), F32)
    for first in range(B - STEP, -1, -STEP):
        delta = deltas(first, first + STEP)
        for b in range(first + STEP - 1, first - 1, -1):
            one = delta[(b - first) * set_count : (b - first + 1) * set_count]
            if at:
                one = one + sofar_ref[b * set_count : (b + 1) * set_count, :]
            carry = rho * carry + weight_ref[b] * one
            quad = quad + (1.0 if b == 0 else 1.0 - rho * rho) * (carry * carry)
    margin = IM_SCALE * jnp.sqrt(1.0 + quad)
    spread = jnp.tanh(set_value / VALUE_SCALE)
    eye = jnp.where(iota((NB, 128), 0) == iota((NB, 128), 1), 1.0, 0.0).astype(BF16)
    basis = dot_nt(eye, states[:, 0:128])
    at = iota(basis.shape, 0)
    basis = jnp.where(at < NF, basis, jnp.where(at == NF, 1.0, 0.0))
    sums = []
    for d in range(DATES):
        own = slice(d * paths, (d + 1) * paths)
        t, m = spread[:, own], margin[:, own]
        some = basis[:, own].astype(BF16)
        ones = jnp.where(iota(some.shape, 0) == NB - 1, 1.0, 0.0).astype(BF16)
        first, second = pieces(jnp.concatenate([t, m], axis=0), 3), pieces(jnp.concatenate([t * t, t * m], axis=0), 3)
        sums.append(sum(dot_nt(some, piece) for piece in first) + sum(dot_nt(ones, piece) for piece in second))
        value_ref[d] = set_value[:, own]
        out_ref[d * set_count : (d + 1) * set_count, :] = set_value[:, own].astype(BF16)
        base = DATES * set_count
        out_ref[base + d * NB : base + (d + 1) * NB, :] = some
    base = DATES * (set_count + NB)
    sums = pieces(jnp.concatenate(sums, axis=1), 3)
    width = 2 * DATES * set_count
    for i, piece in enumerate(sums):
        row, lane = base + i // 2 * NB, i % 2 * width
        out_ref[row : row + NB, lane : lane + width] = piece
    out_ref[base + NB : base + 2 * NB, width : 2 * width] = jnp.zeros((NB, width), BF16)


def fit_kernel(groups, set_count, value_ref, *refs):
    parts, (fit_ref, pos_ref) = refs[:groups], refs[groups:]
    paths = parts[0].shape[1]
    paths_all = groups * paths
    ridge = RIDGE * paths_all
    width = 2 * DATES * set_count
    base = DATES * (set_count + NB)
    total = sum(p[base : base + 2 * NB, :].astype(F32) for p in parts)
    total = total[0:NB, 0:width] + total[0:NB, width : 2 * width] + total[NB : 2 * NB, 0:width]
    shape = (NB, width)
    row = iota(shape, 0)
    shift = 2 * set_count
    bases, sums, works, columns, scales = [], [], [], [], []
    for d in range(DATES):
        first = DATES * set_count + d * NB
        basis = jnp.concatenate([p[first : first + NB, :] for p in parts], axis=1)
        gram = dot_nt(basis, basis)
        gram = jnp.where(iota((NB, NB), 0) == iota((NB, NB), 1), gram + ridge, gram)
        part = pltpu.roll(total, width - d * shift, 1) if d else total
        bases.append(basis)
        sums.append(part)
        works.append(jnp.where(row < NB - 1, part, 0.0))
        columns.append([jnp.broadcast_to(gram[:, j : j + 1], shape) for j in range(NB - 1)])
        scales.append(jnp.zeros(shape, F32))
    for j in range(NB - 1):
        for d in range(DATES):
            column = columns[d]
            inv = 1.0 / jnp.broadcast_to(column[j][j : j + 1, :], shape)
            factor = jnp.where(row == j, 0.0, column[j] * inv)
            scales[d] = jnp.where(row == j, inv, scales[d])
            for k in range(j + 1, NB - 1):
                column[k] = column[k] - factor * jnp.broadcast_to(column[k][j : j + 1, :], shape)
            works[d] = works[d] - factor * jnp.broadcast_to(works[d][j : j + 1, :], shape)
    flats = []
    for d in range(DATES):
        part, basis = sums[d], bases[d]
        right = works[d] * scales[d]
        solved = pltpu.roll(right, width - set_count, 1)
        square = part[NB - 1 : NB] + ridge
        cross = pltpu.roll(part[NB - 1 : NB], width - set_count, 1)
        here = iota((1, width), 1) < set_count
        below = jnp.where(here, square - jnp.sum(part * right, axis=0, keepdims=True), 1.0)
        above = cross - jnp.sum(part * solved, axis=0, keepdims=True)
        slope = jnp.where(here, above / below, 0.0)
        coef = jnp.where(row < NB - 1, solved - right * slope, slope)
        coef = jnp.concatenate([coef, jnp.zeros((width - NB, width), F32)], axis=0).T
        coef = coef[0:set_count]
        values = [value_ref[d]] + [p[d * set_count : (d + 1) * set_count, :].astype(F32) for p in parts[1:]]
        values = jnp.concatenate(values, axis=1)
        linear = sum(dot(piece[:, 0:NB], basis) for piece in pieces(coef, 3))
        fitted = linear + coef[:, NB - 1 : NB] * jnp.tanh(values * (1.0 / VALUE_SCALE))
        fit_ref[d] = fitted[:, 0:paths]
        positive = jnp.sum(jnp.maximum(values - fitted, 0.0), axis=1, keepdims=True)
        flats.append(jnp.broadcast_to(positive * (1.0 / paths_all), (set_count, 128)))
    flats.append(jnp.zeros((128 - DATES * set_count, 128), F32))
    flat = jnp.concatenate(flats, axis=0).T
    for d in range(DATES):
        moved = pltpu.roll(flat, 128 - d * set_count, 1) if d else flat
        pos_ref[d : d + 1, :] = moved[0:1, 0:set_count]


def smem():
    return pl.BlockSpec(memory_space=pltpu.SMEM)


def vmem(count):
    return [pl.BlockSpec(memory_space=pltpu.VMEM)] * count


def params():
    return pltpu.CompilerParams(vmem_limit_bytes=VMEM_LIMIT)


def near(x):
    return pltpu.with_memory_space_constraint(x, pltpu.VMEM)


def turn(x, axis, k):
    n = lax.axis_size(axis)
    return near(lax.ppermute(x, axis, [(i, (i + k) % n) for i in range(n)]))


def meet(x, axis, k):
    n = lax.axis_size(axis)
    return near(lax.ppermute(x, axis, [(i, i ^ k) for i in range(n)]))


def on_device(
    path_states, trade_loads, trade_amounts, trade_legs, trade_set, set_slot, risk_weights
):
    owners = lax.axis_size("trades")
    groups = lax.axis_size("paths")
    trades, factors = trade_loads.shape
    sets = set_slot.shape[0]
    set_count = sets // owners
    cap = 5 * trades // (2 * owners)
    paths = path_states.shape[1]
    cols = DATES * paths
    count = owners * cap
    block = (cap + META, factors)
    few = owners <= 8
    order = ORDER if owners == len(ORDER) else tuple(range(owners))
    me = lax.axis_index("trades").astype(jnp.int32)
    if few:
        shape = [pltpu.VMEM(block, BF16)] * owners
    else:
        me = jnp.zeros_like(me)
        shape = [jax.ShapeDtypeStruct((owners,) + block, BF16)]
    inputs = (
        trade_set.reshape(1, trades),
        set_slot.reshape(1, sets),
        trade_amounts,
        trade_legs,
        trade_loads,
    )
    packed = pl.pallas_call(
        lambda *refs: pack_kernel(owners, order, cap, set_count, *refs),
        out_shape=shape,
        in_specs=[smem()] + [pl.BlockSpec(memory_space=pltpu.HBM)] * 5,
        out_specs=vmem(len(shape)),
        scratch_shapes=[pltpu.VMEM(x.shape, x.dtype) for x in inputs] + [pltpu.SemaphoreType.DMA((5,))],
        compiler_params=params(),
        name="pack",
    )(me.reshape(1), *[pltpu.with_memory_space_constraint(x, pltpu.HBM) for x in inputs])
    states = path_states.reshape(cols, factors)
    reduced = pltpu.VMEM(((B + 1) * set_count, cols), F32)

    def scratch(batch):
        rows = batch * cap
        wide = -(-rows // 128) * 128
        return [
            pltpu.VMEM((rows, cols), F32),
            pltpu.VMEM((2 * wide, cols), BF16),
            pltpu.VMEM((wide, cols), BF16),
            pltpu.VMEM((wide, cols), BF16),
            pltpu.VMEM((B * set_count, 2 * wide), BF16),
        ]

    at, sofar = 0, []
    if few:
        got = [near(packed[0])] + [meet(packed[k], "trades", order[k]) for k in range(1, owners)]
        if owners > EARLY:
            at = EARLY
            sofar = pl.pallas_call(
                lambda *refs: add_kernel(cap, set_count, *refs),
                out_shape=[reduced],
                in_specs=vmem(1 + at),
                out_specs=vmem(1),
                scratch_shapes=scratch(at),
                compiler_params=params(),
                name="add",
            )(states, *got[:at])
            sofar = [near(sofar[0])]
        last, held = got[at:], owners - at
    else:
        last, held = [lax.all_to_all(packed[0], "trades", split_axis=0, concat_axis=0, tiled=True)], owners
    packet = (DATES * (set_count + NB) + 2 * NB, paths)
    mine, value = pl.pallas_call(
        lambda *refs: owner_kernel(owners, at, cap, set_count, *refs),
        out_shape=[
            pltpu.VMEM(packet, BF16),
            pltpu.VMEM((DATES, set_count, paths), F32),
        ],
        in_specs=[smem()] + vmem(1 + len(sofar) + len(last)),
        out_specs=vmem(2),
        scratch_shapes=scratch(held),
        compiler_params=params(),
        name="owner",
    )(risk_weights, states, *sofar, *last)
    parts = [near(mine)] + [meet(mine, "paths", k) for k in range(1, groups)]
    fitted_margin, exposure = pl.pallas_call(
        lambda *refs: fit_kernel(groups, set_count, *refs),
        out_shape=[
            jax.ShapeDtypeStruct((DATES, set_count, paths), F32),
            jax.ShapeDtypeStruct((DATES, set_count), F32),
        ],
        in_specs=vmem(1 + groups),
        out_specs=vmem(2),
        compiler_params=params(),
        name="fit",
    )(near(value), *parts)
    return (fitted_margin, exposure)


def solution(mesh):
    in_specs = (
        P(None, "paths", None),
        P("trades", None),
        P(None, "trades"),
        P(None, "trades"),
        P("trades"),
        P(),
        P(),
    )
    out_specs = (P(None, "trades", "paths"), P(None, "trades"))
    return jax.shard_map(
        on_device, mesh=mesh, in_specs=in_specs, out_specs=out_specs, check_vma=False
    )
```

```python
import math

import jax
import jax.numpy as jnp
from jax import lax
from jax.experimental import pallas as pl
from jax.experimental.pallas import tpu as pltpu
from jax.sharding import PartitionSpec as P

B = 40
NB = 16
DATES = 2
NF = NB - 2
META = 8
EARLY = 5
ORDER = (0, 2, 4, 3, 1, 5, 6, 7)
STEP = 4
HALF = 256

CORR_LEN = 8.0
IM_SCALE = 0.2
RIDGE = 0.05
VALUE_SCALE = 4.0

F32 = jnp.float32
BF16 = jnp.bfloat16
VMEM_LIMIT = 40 << 20
NT = (((1,), (1,)), ((), ()))


def iota(shape, axis):
    return lax.broadcasted_iota(jnp.int32, shape, axis)


def dot(a, b):
    return jnp.dot(a, b, preferred_element_type=F32)


def dot_nt(a, b):
    return lax.dot_general(a, b, NT, preferred_element_type=F32)


def pieces(x, count):
    out = []
    for _ in range(count):
        piece = x.astype(BF16)
        out.append(piece)
        x = x - piece.astype(F32)
    return out


def pick_rows(rows, height):
    width = rows[0].shape[1]
    at = iota((height, width), 0)
    out = jnp.zeros((height, width), F32)
    for i, row in enumerate(rows):
        out = jnp.where(at == i, row, out)
    return out


def pack_kernel(owners, order, cap, set_count, me_ref, *refs):
    outs, held, arrived = refs[5:-6], refs[-6:-1], refs[-1]
    copies = [pltpu.make_async_copy(refs[i], held[i], arrived.at[i]) for i in range(5)]
    for copy in copies:
        copy.start()
    set_ref, slot_ref, amount_ref, leg_ref, load_ref = held
    for copy in copies[:4]:
        copy.wait()
    trades = set_ref.shape[1]
    sets = slot_ref.shape[1]
    slot = slot_ref[...].astype(F32)
    slot_owner = jnp.floor((slot + 0.5) * (1.0 / set_count))
    slot_local = slot - slot_owner * set_count
    digits = pick_rows([slot_owner, slot_local], 16).astype(BF16)
    member = jnp.where(iota((sets, trades), 0) == set_ref[...], 1.0, 0.0).astype(BF16)
    found = dot(digits, member)
    owner, local = found[0:1], found[1:2]
    height = -(-owners // 16) * 16
    marks = jnp.where(iota((height, trades), 0).astype(F32) == owner, 1.0, 0.0)
    ahead = jnp.where(iota((trades, trades), 0) < iota((trades, trades), 1), 1.0, 0.0).astype(BF16)
    rank = jnp.sum(dot(marks.astype(BF16), ahead) * marks, axis=0, keepdims=True)
    target = (owner * cap + rank).astype(jnp.int32)
    amounts = amount_ref[...]
    legs = leg_ref[...].astype(F32)
    meta = [p.astype(F32) for p in pieces(amounts[0:1], 3) + pieces(amounts[1:2], 3)]
    meta = pick_rows(meta + [legs[0:1], legs[1:2], local], 16).astype(BF16)
    copies[4].wait()
    group = 8 if owners > 8 else owners
    for base in range(0, owners, group):
        chosen, places = range(base, base + group), []
        for k in chosen:
            spot = target - (me_ref[0] ^ order[k]) * cap
            spot = jnp.where((spot >= 0) & (spot < cap), spot + (k * cap) % 128, -1)
            places.append(jnp.where(iota((HALF, trades), 0) == spot, 1.0, 0.0).astype(BF16))
        aligned = (group * cap) % 128 == 0 and cap % 16 == 0
        if aligned:
            rows = [p[(k * cap) % 128 : (k * cap) % 128 + cap] for k, p in zip(chosen, places)]
            moved = dot(jnp.concatenate(rows, axis=0), load_ref[...])
        for i, k in enumerate(chosen):
            tags = dot_nt(meta, places[i]).astype(BF16)
            out = outs[k] if len(outs) > 1 else outs[0].at[k]
            if aligned:
                out[0:cap, :] = moved[i * cap : (i + 1) * cap].astype(BF16)
            else:
                whole = dot(places[i], load_ref[...])
                out[0:cap, :] = whole[(k * cap) % 128 : (k * cap) % 128 + cap].astype(BF16)
            out[cap : cap + META, 0:HALF] = tags[0:META]
            out[cap : cap + META, HALF : 2 * HALF] = tags[META : 2 * META]


def side_by_side(blocks, at, cap, width):
    start = at * cap // 128 * 128
    tiles = [None] * (width // 128 + 2)
    for i, block in enumerate(blocks):
        first = ((at + i) * cap - start) // 128
        for j in range(HALF // 128):
            low = block[cap : cap + META, j * 128 : (j + 1) * 128]
            high = block[cap : cap + META, HALF + j * 128 : HALF + (j + 1) * 128]
            tile = jnp.concatenate([low, high], axis=0).astype(F32)
            tiles[first + j] = tile if tiles[first + j] is None else tiles[first + j] + tile
    tiles = [jnp.zeros((2 * META, 128), F32) if t is None else t for t in tiles]
    shift = at * cap - start
    if not shift:
        return jnp.concatenate(tiles[: width // 128], axis=1)
    meta = jnp.concatenate(tiles, axis=1)
    return pltpu.roll(meta, meta.shape[1] - shift, 1)[:, :width]


def price(blocks, at, cap, set_count, states, scratch):
    level_ref, terms_ref, high_ref, low_ref, place_ref = scratch
    count = len(blocks) * cap
    width = high_ref.shape[0]
    loads = jnp.concatenate([block[0:cap, :] for block in blocks], axis=0)
    level_ref[...] = dot_nt(loads, states)
    meta = side_by_side(blocks, at, cap, width)
    eye = jnp.where(iota((16, 128), 0) % 2 == iota((16, 128), 1), 1.0, 0.0).astype(BF16)
    turned = pick_rows([meta[i : i + 1] for i in (0, 3, 1, 4, 2, 5)], 16).astype(BF16)
    columns = lax.dot_general(turned, eye, (((0,), (0,)), ((), ())), preferred_element_type=F32)
    step = math.gcd(count, 128)
    for r in range(0, count, step):
        x = level_ref[r : r + step, :]
        a = columns[r : r + step, 0:1]
        c = columns[r : r + step, 1:2]
        e = jnp.exp(-jnp.abs(x))
        more = 1.0 + e
        tail = jnp.log(more)
        near = 1.0 / more
        far = e * near
        up = x >= 0.0
        value = a * (jnp.maximum(x, 0.0) + tail) + c * (jnp.maximum(-x, 0.0) + tail)
        terms_ref[r : r + step, :] = (a * jnp.where(up, near, far)).astype(BF16)
        terms_ref[width + r : width + r + step, :] = (-c * jnp.where(up, far, near)).astype(BF16)
        high = value.astype(BF16)
        high_ref[r : r + step, :] = high
        low_ref[r : r + step, :] = (value - high.astype(F32)).astype(BF16)
    if width > count:
        for ref, first in ((terms_ref, 0), (terms_ref, width), (high_ref, 0), (low_ref, 0)):
            ref[first + count : first + width, :] = jnp.zeros((width - count, ref.shape[1]), BF16)
    in_set = jnp.where(iota((set_count, width), 0).astype(F32) == meta[8:9], 1.0, 0.0)

    def bucket_deltas(first, last):
        rows = slice(first * set_count, last * set_count)
        for leg in range(2):
            for b in range(first, last):
                place_ref[b * set_count : (b + 1) * set_count, leg * width : (leg + 1) * width] = (
                    jnp.where(meta[6 + leg : 7 + leg] == float(b), in_set, 0.0).astype(BF16)
                )
        return dot(place_ref[rows, :], terms_ref[...])

    named = in_set.astype(BF16)
    return bucket_deltas, dot(named, high_ref[...]) + dot(named, low_ref[...])


def add_kernel(cap, set_count, state_ref, *refs):
    scratch, out_ref, blocks = refs[-5:], refs[-6], refs[:-6]
    deltas, value = price(blocks, 0, cap, set_count, state_ref[...], scratch)
    for b in range(0, B, STEP):
        out_ref[b * set_count : (b + STEP) * set_count, :] = deltas(b, b + STEP)
    out_ref[B * set_count :, :] = value


def owner_kernel(owners, at, cap, set_count, weight_ref, state_ref, *refs):
    out_ref, value_ref = refs[-7:-5]
    blocks = refs[1:-7] if at else refs[:-7]
    sofar_ref = refs[0]
    if len(blocks) == 1 and owners > 1:
        blocks = [blocks[0].at[k] for k in range(owners)]
    cols = state_ref.shape[0]
    paths = cols // DATES
    states = state_ref[...]
    deltas, set_value = price(blocks, at, cap, set_count, states, refs[-5:])
    if at:
        set_value = set_value + sofar_ref[B * set_count :, :]
    rho = math.exp(-1.0 / CORR_LEN)
    carry = jnp.zeros((set_count, cols), F32)
    quad = jnp.zeros((set_count, cols), F32)
    for first in range(B - STEP, -1, -STEP):
        delta = deltas(first, first + STEP)
        for b in range(first + STEP - 1, first - 1, -1):
            one = delta[(b - first) * set_count : (b - first + 1) * set_count]
            if at:
                one = one + sofar_ref[b * set_count : (b + 1) * set_count, :]
            carry = rho * carry + jnp.broadcast_to(weight_ref[0:1, b : b + 1], one.shape) * one
            quad = quad + (1.0 if b == 0 else 1.0 - rho * rho) * (carry * carry)
    margin = IM_SCALE * jnp.sqrt(1.0 + quad)
    spread = jnp.tanh(set_value / VALUE_SCALE)
    eye = jnp.where(iota((NB, 128), 0) == iota((NB, 128), 1), 1.0, 0.0).astype(BF16)
    basis = dot_nt(eye, states[:, 0:128])
    at = iota(basis.shape, 0)
    basis = jnp.where(at < NF, basis, jnp.where(at == NF, 1.0, 0.0))
    sums = []
    for d in range(DATES):
        own = slice(d * paths, (d + 1) * paths)
        t, m = spread[:, own], margin[:, own]
        some = basis[:, own].astype(BF16)
        ones = jnp.where(iota(some.shape, 0) == NB - 1, 1.0, 0.0).astype(BF16)
        first, second = pieces(jnp.concatenate([t, m], axis=0), 3), pieces(jnp.concatenate([t * t, t * m], axis=0), 3)
        sums.append(sum(dot_nt(some, piece) for piece in first) + sum(dot_nt(ones, piece) for piece in second))
        value_ref[d] = set_value[:, own]
        out_ref[d * set_count : (d + 1) * set_count, :] = set_value[:, own].astype(BF16)
        base = DATES * set_count
        out_ref[base + d * NB : base + (d + 1) * NB, :] = some
    base = DATES * (set_count + NB)
    sums = pieces(jnp.concatenate(sums, axis=1), 3)
    width = 2 * DATES * set_count
    out_ref[base : base + NB, 0:width] = sums[0]
    out_ref[base : base + NB, width : 2 * width] = sums[1]
    half = NB // 2
    out_ref[base + NB : base + NB + half, 0:width] = sums[2][0:half]
    out_ref[base + NB : base + NB + half, width : 2 * width] = sums[2][half:NB]


def fit_kernel(groups, set_count, value_ref, *refs):
    parts, (fit_ref, pos_ref) = refs[:groups], refs[groups:]
    paths = parts[0].shape[1]
    paths_all = groups * paths
    ridge = RIDGE * paths_all
    width = 2 * DATES * set_count
    base = DATES * (set_count + NB)
    rest = sum(p[base + NB : base + NB + NB // 2, :].astype(F32) for p in parts)
    total = sum(p[base : base + NB, :].astype(F32) for p in parts)
    total = total[:, 0:width] + total[:, width : 2 * width]
    total = total + jnp.concatenate([rest[:, 0:width], rest[:, width : 2 * width]], axis=0)
    shape = (NB, width)
    row = iota(shape, 0)
    shift = 2 * set_count
    bases, sums, works, columns, scales = [], [], [], [], []
    for d in range(DATES):
        first = DATES * set_count + d * NB
        basis = jnp.concatenate([p[first : first + NB, :] for p in parts], axis=1)
        gram = dot_nt(basis, basis)
        gram = jnp.where(iota((NB, NB), 0) == iota((NB, NB), 1), gram + ridge, gram)
        part = pltpu.roll(total, width - d * shift, 1) if d else total
        bases.append(basis)
        sums.append(part)
        works.append(jnp.where(row < NB - 1, part, 0.0))
        columns.append([jnp.broadcast_to(gram[:, j : j + 1], shape) for j in range(NB - 1)])
        scales.append(jnp.zeros(shape, F32))
    for j in range(NB - 1):
        for d in range(DATES):
            column = columns[d]
            inv = 1.0 / jnp.broadcast_to(column[j][j : j + 1, :], shape)
            factor = jnp.where(row == j, 0.0, column[j] * inv)
            scales[d] = jnp.where(row == j, inv, scales[d])
            for k in range(j + 1, NB - 1):
                column[k] = column[k] - factor * jnp.broadcast_to(column[k][j : j + 1, :], shape)
            works[d] = works[d] - factor * jnp.broadcast_to(works[d][j : j + 1, :], shape)
    flats = []
    for d in range(DATES):
        part, basis = sums[d], bases[d]
        right = works[d] * scales[d]
        solved = pltpu.roll(right, width - set_count, 1)
        square = part[NB - 1 : NB] + ridge
        cross = pltpu.roll(part[NB - 1 : NB], width - set_count, 1)
        here = iota((1, width), 1) < set_count
        below = jnp.where(here, square - jnp.sum(part * right, axis=0, keepdims=True), 1.0)
        above = cross - jnp.sum(part * solved, axis=0, keepdims=True)
        slope = jnp.where(here, above / below, 0.0)
        coef = jnp.where(row < NB - 1, solved - right * slope, slope)
        coef = jnp.concatenate([coef, jnp.zeros((width - NB, width), F32)], axis=0).T
        coef = coef[0:set_count]
        values = [value_ref[d]] + [p[d * set_count : (d + 1) * set_count, :].astype(F32) for p in parts[1:]]
        values = jnp.concatenate(values, axis=1)
        linear = sum(dot(piece[:, 0:NB], basis) for piece in pieces(coef, 3))
        fitted = linear + coef[:, NB - 1 : NB] * jnp.tanh(values * (1.0 / VALUE_SCALE))
        fit_ref[d] = fitted[:, 0:paths]
        positive = jnp.sum(jnp.maximum(values - fitted, 0.0), axis=1, keepdims=True)
        flats.append(jnp.broadcast_to(positive * (1.0 / paths_all), (set_count, 128)))
    flats.append(jnp.zeros((128 - DATES * set_count, 128), F32))
    flat = jnp.concatenate(flats, axis=0).T
    for d in range(DATES):
        moved = pltpu.roll(flat, 128 - d * set_count, 1) if d else flat
        pos_ref[d : d + 1, :] = moved[0:1, 0:set_count]


def smem():
    return pl.BlockSpec(memory_space=pltpu.SMEM)


def vmem(count):
    return [pl.BlockSpec(memory_space=pltpu.VMEM)] * count


def params():
    return pltpu.CompilerParams(vmem_limit_bytes=VMEM_LIMIT)


def near(x):
    return pltpu.with_memory_space_constraint(x, pltpu.VMEM)


def turn(x, axis, k):
    n = lax.axis_size(axis)
    return near(lax.ppermute(x, axis, [(i, (i + k) % n) for i in range(n)]))


def meet(x, axis, k):
    n = lax.axis_size(axis)
    return near(lax.ppermute(x, axis, [(i, i ^ k) for i in range(n)]))


def on_device(
    path_states, trade_loads, trade_amounts, trade_legs, trade_set, set_slot, risk_weights
):
    owners = lax.axis_size("trades")
    groups = lax.axis_size("paths")
    trades, factors = trade_loads.shape
    sets = set_slot.shape[0]
    set_count = sets // owners
    cap = 5 * trades // (2 * owners)
    paths = path_states.shape[1]
    cols = DATES * paths
    count = owners * cap
    block = (cap + META, factors)
    few = owners <= 8
    order = ORDER if owners == len(ORDER) else tuple(range(owners))
    me = lax.axis_index("trades").astype(jnp.int32)
    if few:
        shape = [pltpu.VMEM(block, BF16)] * owners
    else:
        me = jnp.zeros_like(me)
        shape = [jax.ShapeDtypeStruct((owners,) + block, BF16)]
    inputs = (
        trade_set.reshape(1, trades),
        set_slot.reshape(1, sets),
        trade_amounts,
        trade_legs,
        trade_loads,
    )
    packed = pl.pallas_call(
        lambda *refs: pack_kernel(owners, order, cap, set_count, *refs),
        out_shape=shape,
        in_specs=[smem()] + [pl.BlockSpec(memory_space=pltpu.HBM)] * 5,
        out_specs=vmem(len(shape)),
        scratch_shapes=[pltpu.VMEM(x.shape, x.dtype) for x in inputs] + [pltpu.SemaphoreType.DMA((5,))],
        compiler_params=params(),
        name="pack",
    )(me.reshape(1), *[pltpu.with_memory_space_constraint(x, pltpu.HBM) for x in inputs])
    states = path_states.reshape(cols, factors)
    reduced = pltpu.VMEM(((B + 1) * set_count, cols), F32)

    def scratch(batch):
        rows = batch * cap
        wide = -(-rows // 128) * 128
        return [
            pltpu.VMEM((rows, cols), F32),
            pltpu.VMEM((2 * wide, cols), BF16),
            pltpu.VMEM((wide, cols), BF16),
            pltpu.VMEM((wide, cols), BF16),
            pltpu.VMEM((B * set_count, 2 * wide), BF16),
        ]

    at, sofar = 0, []
    if few:
        got = [near(packed[0])] + [meet(packed[k], "trades", order[k]) for k in range(1, owners)]
        if owners > EARLY:
            at = EARLY
            sofar = pl.pallas_call(
                lambda *refs: add_kernel(cap, set_count, *refs),
                out_shape=[reduced],
                in_specs=vmem(1 + at),
                out_specs=vmem(1),
                scratch_shapes=scratch(at),
                compiler_params=params(),
                name="add",
            )(states, *got[:at])
            sofar = [near(sofar[0])]
        last, held = got[at:], owners - at
    else:
        last, held = [lax.all_to_all(packed[0], "trades", split_axis=0, concat_axis=0, tiled=True)], owners
    packet = (DATES * (set_count + NB) + NB + NB // 2, paths)
    mine, value = pl.pallas_call(
        lambda *refs: owner_kernel(owners, at, cap, set_count, *refs),
        out_shape=[
            pltpu.VMEM(packet, BF16),
            pltpu.VMEM((DATES, set_count, paths), F32),
        ],
        in_specs=vmem(2 + len(sofar) + len(last)),
        out_specs=vmem(2),
        scratch_shapes=scratch(held),
        compiler_params=params(),
        name="owner",
    )(near(risk_weights.reshape(1, B)), states, *sofar, *last)
    parts = [near(mine)] + [meet(mine, "paths", k) for k in range(1, groups)]
    fitted_margin, exposure = pl.pallas_call(
        lambda *refs: fit_kernel(groups, set_count, *refs),
        out_shape=[
            jax.ShapeDtypeStruct((DATES, set_count, paths), F32),
            jax.ShapeDtypeStruct((DATES, set_count), F32),
        ],
        in_specs=vmem(1 + groups),
        out_specs=vmem(2),
        compiler_params=params(),
        name="fit",
    )(near(value), *parts)
    return (fitted_margin, exposure)


def solution(mesh):
    in_specs = (
        P(None, "paths", None),
        P("trades", None),
        P(None, "trades"),
        P(None, "trades"),
        P("trades"),
        P(),
        P(),
    )
    out_specs = (P(None, "trades", "paths"), P(None, "trades"))
    return jax.shard_map(
        on_device, mesh=mesh, in_specs=in_specs, out_specs=out_specs, check_vma=False
    )
```

```python
import math

import jax
import jax.numpy as jnp
from jax import lax
from jax.experimental import pallas as pl
from jax.experimental.pallas import tpu as pltpu
from jax.sharding import PartitionSpec as P

B = 40
NB = 16
DATES = 2
NF = NB - 2
META = 8
EARLY = 5
ORDER = (0, 2, 4, 3, 1, 5, 6, 7)
STEP = 5
HALF = 256

CORR_LEN = 8.0
IM_SCALE = 0.2
RIDGE = 0.05
VALUE_SCALE = 4.0

F32 = jnp.float32
BF16 = jnp.bfloat16
VMEM_LIMIT = 40 << 20
NT = (((1,), (1,)), ((), ()))


def iota(shape, axis):
    return lax.broadcasted_iota(jnp.int32, shape, axis)


def dot(a, b):
    return jnp.dot(a, b, preferred_element_type=F32)


def dot_nt(a, b):
    return lax.dot_general(a, b, NT, preferred_element_type=F32)


def pieces(x, count):
    out = []
    for _ in range(count):
        piece = x.astype(BF16)
        out.append(piece)
        x = x - piece.astype(F32)
    return out


def pick_rows(rows, height):
    width = rows[0].shape[1]
    at = iota((height, width), 0)
    out = jnp.zeros((height, width), F32)
    for i, row in enumerate(rows):
        out = jnp.where(at == i, row, out)
    return out


def pack_kernel(owners, order, cap, set_count, me_ref, *refs):
    outs, held, arrived = refs[5:-6], refs[-6:-1], refs[-1]
    copies = [pltpu.make_async_copy(refs[i], held[i], arrived.at[i]) for i in range(5)]
    for copy in copies:
        copy.start()
    set_ref, slot_ref, amount_ref, leg_ref, load_ref = held
    for copy in copies[:4]:
        copy.wait()
    trades = set_ref.shape[1]
    sets = slot_ref.shape[1]
    slot = slot_ref[...].astype(F32)
    slot_owner = jnp.floor((slot + 0.5) * (1.0 / set_count))
    slot_local = slot - slot_owner * set_count
    digits = pick_rows([slot_owner, slot_local], 16).astype(BF16)
    member = jnp.where(iota((sets, trades), 0) == set_ref[...], 1.0, 0.0).astype(BF16)
    found = dot(digits, member)
    owner, local = found[0:1], found[1:2]
    height = -(-owners // 16) * 16
    marks = jnp.where(iota((height, trades), 0).astype(F32) == owner, 1.0, 0.0)
    ahead = jnp.where(iota((trades, trades), 0) < iota((trades, trades), 1), 1.0, 0.0).astype(BF16)
    rank = jnp.sum(dot(marks.astype(BF16), ahead) * marks, axis=0, keepdims=True)
    target = (owner * cap + rank).astype(jnp.int32)
    amounts = amount_ref[...]
    legs = leg_ref[...].astype(F32)
    meta = [p.astype(F32) for p in pieces(amounts[0:1], 3) + pieces(amounts[1:2], 3)]
    meta = pick_rows(meta + [legs[0:1], legs[1:2], local], 16).astype(BF16)
    copies[4].wait()
    group = 8 if owners > 8 else owners
    for base in range(0, owners, group):
        chosen, places = range(base, base + group), []
        for k in chosen:
            spot = target - (me_ref[0] ^ order[k]) * cap
            spot = jnp.where((spot >= 0) & (spot < cap), spot + (k * cap) % 128, -1)
            places.append(jnp.where(iota((HALF, trades), 0) == spot, 1.0, 0.0).astype(BF16))
        aligned = (group * cap) % 128 == 0 and cap % 16 == 0
        if aligned:
            rows = [p[(k * cap) % 128 : (k * cap) % 128 + cap] for k, p in zip(chosen, places)]
            moved = dot(jnp.concatenate(rows, axis=0), load_ref[...])
        for i, k in enumerate(chosen):
            tags = dot_nt(meta, places[i]).astype(BF16)
            out = outs[k] if len(outs) > 1 else outs[0].at[k]
            if aligned:
                out[0:cap, :] = moved[i * cap : (i + 1) * cap].astype(BF16)
            else:
                whole = dot(places[i], load_ref[...])
                out[0:cap, :] = whole[(k * cap) % 128 : (k * cap) % 128 + cap].astype(BF16)
            out[cap : cap + META, 0:HALF] = tags[0:META]
            out[cap : cap + META, HALF : 2 * HALF] = tags[META : 2 * META]


def side_by_side(blocks, at, cap, width):
    start = at * cap // 128 * 128
    tiles = [None] * (width // 128 + 2)
    for i, block in enumerate(blocks):
        first = ((at + i) * cap - start) // 128
        for j in range(HALF // 128):
            low = block[cap : cap + META, j * 128 : (j + 1) * 128]
            high = block[cap : cap + META, HALF + j * 128 : HALF + (j + 1) * 128]
            tile = jnp.concatenate([low, high], axis=0).astype(F32)
            tiles[first + j] = tile if tiles[first + j] is None else tiles[first + j] + tile
    tiles = [jnp.zeros((2 * META, 128), F32) if t is None else t for t in tiles]
    shift = at * cap - start
    if not shift:
        return jnp.concatenate(tiles[: width // 128], axis=1)
    meta = jnp.concatenate(tiles, axis=1)
    return pltpu.roll(meta, meta.shape[1] - shift, 1)[:, :width]


def price(blocks, at, cap, set_count, states, scratch):
    level_ref, terms_ref, high_ref, low_ref, place_ref = scratch
    count = len(blocks) * cap
    width = high_ref.shape[0]
    loads = jnp.concatenate([block[0:cap, :] for block in blocks], axis=0)
    level_ref[...] = dot_nt(loads, states)
    meta = side_by_side(blocks, at, cap, width)
    eye = jnp.where(iota((16, 128), 0) % 2 == iota((16, 128), 1), 1.0, 0.0).astype(BF16)
    turned = pick_rows([meta[i : i + 1] for i in (0, 3, 1, 4, 2, 5)], 16).astype(BF16)
    columns = lax.dot_general(turned, eye, (((0,), (0,)), ((), ())), preferred_element_type=F32)
    step = math.gcd(count, 128)
    for r in range(0, count, step):
        x = level_ref[r : r + step, :]
        a = columns[r : r + step, 0:1]
        c = columns[r : r + step, 1:2]
        e = jnp.exp(-jnp.abs(x))
        more = 1.0 + e
        tail = jnp.log(more)
        near = 1.0 / more
        far = e * near
        up = x >= 0.0
        value = a * (jnp.maximum(x, 0.0) + tail) + c * (jnp.maximum(-x, 0.0) + tail)
        terms_ref[r : r + step, :] = (a * jnp.where(up, near, far)).astype(BF16)
        terms_ref[width + r : width + r + step, :] = (-c * jnp.where(up, far, near)).astype(BF16)
        high = value.astype(BF16)
        high_ref[r : r + step, :] = high
        low_ref[r : r + step, :] = (value - high.astype(F32)).astype(BF16)
    if width > count:
        for ref, first in ((terms_ref, 0), (terms_ref, width), (high_ref, 0), (low_ref, 0)):
            ref[first + count : first + width, :] = jnp.zeros((width - count, ref.shape[1]), BF16)
    in_set = jnp.where(iota((set_count, width), 0).astype(F32) == meta[8:9], 1.0, 0.0)

    def bucket_deltas(first, last):
        rows = slice(first * set_count, last * set_count)
        for leg in range(2):
            for b in range(first, last):
                place_ref[b * set_count : (b + 1) * set_count, leg * width : (leg + 1) * width] = (
                    jnp.where(meta[6 + leg : 7 + leg] == float(b), in_set, 0.0).astype(BF16)
                )
        return dot(place_ref[rows, :], terms_ref[...])

    named = in_set.astype(BF16)
    return bucket_deltas, dot(named, high_ref[...]) + dot(named, low_ref[...])


def add_kernel(cap, set_count, state_ref, *refs):
    scratch, out_ref, blocks = refs[-5:], refs[-6], refs[:-6]
    deltas, value = price(blocks, 0, cap, set_count, state_ref[...], scratch)
    for b in range(0, B, STEP):
        out_ref[b * set_count : (b + STEP) * set_count, :] = deltas(b, b + STEP)
    out_ref[B * set_count :, :] = value


def owner_kernel(owners, at, cap, set_count, weight_ref, state_ref, *refs):
    out_ref, value_ref = refs[-7:-5]
    blocks = refs[1:-7] if at else refs[:-7]
    sofar_ref = refs[0]
    if len(blocks) == 1 and owners > 1:
        blocks = [blocks[0].at[k] for k in range(owners)]
    cols = state_ref.shape[0]
    paths = cols // DATES
    states = state_ref[...]
    deltas, set_value = price(blocks, at, cap, set_count, states, refs[-5:])
    if at:
        set_value = set_value + sofar_ref[B * set_count :, :]
    rho = math.exp(-1.0 / CORR_LEN)
    carry = jnp.zeros((set_count, cols), F32)
    quad = jnp.zeros((set_count, cols), F32)
    for first in range(B - STEP, -1, -STEP):
        delta = deltas(first, first + STEP)
        for b in range(first + STEP - 1, first - 1, -1):
            one = delta[(b - first) * set_count : (b - first + 1) * set_count]
            if at:
                one = one + sofar_ref[b * set_count : (b + 1) * set_count, :]
            carry = rho * carry + jnp.broadcast_to(weight_ref[0:1, b : b + 1], one.shape) * one
            quad = quad + (1.0 if b == 0 else 1.0 - rho * rho) * (carry * carry)
    margin = IM_SCALE * jnp.sqrt(1.0 + quad)
    spread = jnp.tanh(set_value / VALUE_SCALE)
    eye = jnp.where(iota((NB, 128), 0) == iota((NB, 128), 1), 1.0, 0.0).astype(BF16)
    basis = dot_nt(eye, states[:, 0:128])
    at = iota(basis.shape, 0)
    basis = jnp.where(at < NF, basis, jnp.where(at == NF, 1.0, 0.0))
    sums = []
    for d in range(DATES):
        own = slice(d * paths, (d + 1) * paths)
        t, m = spread[:, own], margin[:, own]
        some = basis[:, own].astype(BF16)
        ones = jnp.where(iota(some.shape, 0) == NB - 1, 1.0, 0.0).astype(BF16)
        first, second = pieces(jnp.concatenate([t, m], axis=0), 3), pieces(jnp.concatenate([t * t, t * m], axis=0), 3)
        sums.append(sum(dot_nt(some, piece) for piece in first) + sum(dot_nt(ones, piece) for piece in second))
        value_ref[d] = set_value[:, own]
        out_ref[d * set_count : (d + 1) * set_count, :] = set_value[:, own].astype(BF16)
        base = DATES * set_count
        out_ref[base + d * NB : base + (d + 1) * NB, :] = some
    base = DATES * (set_count + NB)
    sums = pieces(jnp.concatenate(sums, axis=1), 3)
    width = 2 * DATES * set_count
    out_ref[base : base + NB, 0:width] = sums[0]
    out_ref[base : base + NB, width : 2 * width] = sums[1]
    half = NB // 2
    out_ref[base + NB : base + NB + half, 0:width] = sums[2][0:half]
    out_ref[base + NB : base + NB + half, width : 2 * width] = sums[2][half:NB]


def fit_kernel(groups, set_count, value_ref, *refs):
    parts, (fit_ref, pos_ref) = refs[:groups], refs[groups:]
    paths = parts[0].shape[1]
    paths_all = groups * paths
    ridge = RIDGE * paths_all
    width = 2 * DATES * set_count
    base = DATES * (set_count + NB)
    rest = sum(p[base + NB : base + NB + NB // 2, :].astype(F32) for p in parts)
    total = sum(p[base : base + NB, :].astype(F32) for p in parts)
    total = total[:, 0:width] + total[:, width : 2 * width]
    total = total + jnp.concatenate([rest[:, 0:width], rest[:, width : 2 * width]], axis=0)
    shape = (NB, width)
    row = iota(shape, 0)
    shift = 2 * set_count
    bases, sums, works, columns, scales = [], [], [], [], []
    for d in range(DATES):
        first = DATES * set_count + d * NB
        basis = jnp.concatenate([p[first : first + NB, :] for p in parts], axis=1)
        gram = dot_nt(basis, basis)
        gram = jnp.where(iota((NB, NB), 0) == iota((NB, NB), 1), gram + ridge, gram)
        part = pltpu.roll(total, width - d * shift, 1) if d else total
        bases.append(basis)
        sums.append(part)
        works.append(jnp.where(row < NB - 1, part, 0.0))
        columns.append([jnp.broadcast_to(gram[:, j : j + 1], shape) for j in range(NB - 1)])
        scales.append(jnp.zeros(shape, F32))
    for j in range(NB - 1):
        for d in range(DATES):
            column = columns[d]
            inv = 1.0 / jnp.broadcast_to(column[j][j : j + 1, :], shape)
            factor = jnp.where(row == j, 0.0, column[j] * inv)
            scales[d] = jnp.where(row == j, inv, scales[d])
            for k in range(j + 1, NB - 1):
                column[k] = column[k] - factor * jnp.broadcast_to(column[k][j : j + 1, :], shape)
            works[d] = works[d] - factor * jnp.broadcast_to(works[d][j : j + 1, :], shape)
    flats = []
    for d in range(DATES):
        part, basis = sums[d], bases[d]
        right = works[d] * scales[d]
        solved = pltpu.roll(right, width - set_count, 1)
        square = part[NB - 1 : NB] + ridge
        cross = pltpu.roll(part[NB - 1 : NB], width - set_count, 1)
        here = iota((1, width), 1) < set_count
        below = jnp.where(here, square - jnp.sum(part * right, axis=0, keepdims=True), 1.0)
        above = cross - jnp.sum(part * solved, axis=0, keepdims=True)
        slope = jnp.where(here, above / below, 0.0)
        coef = jnp.where(row < NB - 1, solved - right * slope, slope)
        coef = jnp.concatenate([coef, jnp.zeros((width - NB, width), F32)], axis=0).T
        coef = coef[0:set_count]
        values = [value_ref[d]] + [p[d * set_count : (d + 1) * set_count, :].astype(F32) for p in parts[1:]]
        values = jnp.concatenate(values, axis=1)
        linear = sum(dot(piece[:, 0:NB], basis) for piece in pieces(coef, 3))
        fitted = linear + coef[:, NB - 1 : NB] * jnp.tanh(values * (1.0 / VALUE_SCALE))
        fit_ref[d] = fitted[:, 0:paths]
        positive = jnp.sum(jnp.maximum(values - fitted, 0.0), axis=1, keepdims=True)
        flats.append(jnp.broadcast_to(positive * (1.0 / paths_all), (set_count, 128)))
    flats.append(jnp.zeros((128 - DATES * set_count, 128), F32))
    flat = jnp.concatenate(flats, axis=0).T
    for d in range(DATES):
        moved = pltpu.roll(flat, 128 - d * set_count, 1) if d else flat
        pos_ref[d : d + 1, :] = moved[0:1, 0:set_count]


def smem():
    return pl.BlockSpec(memory_space=pltpu.SMEM)


def vmem(count):
    return [pl.BlockSpec(memory_space=pltpu.VMEM)] * count


def params():
    return pltpu.CompilerParams(vmem_limit_bytes=VMEM_LIMIT)


def near(x):
    return pltpu.with_memory_space_constraint(x, pltpu.VMEM)


def turn(x, axis, k):
    n = lax.axis_size(axis)
    return near(lax.ppermute(x, axis, [(i, (i + k) % n) for i in range(n)]))


def meet(x, axis, k):
    n = lax.axis_size(axis)
    return near(lax.ppermute(x, axis, [(i, i ^ k) for i in range(n)]))


def on_device(
    path_states, trade_loads, trade_amounts, trade_legs, trade_set, set_slot, risk_weights
):
    owners = lax.axis_size("trades")
    groups = lax.axis_size("paths")
    trades, factors = trade_loads.shape
    sets = set_slot.shape[0]
    set_count = sets // owners
    cap = 5 * trades // (2 * owners)
    paths = path_states.shape[1]
    cols = DATES * paths
    count = owners * cap
    block = (cap + META, factors)
    few = owners <= 8
    order = ORDER if owners == len(ORDER) else tuple(range(owners))
    me = lax.axis_index("trades").astype(jnp.int32)
    if few:
        shape = [pltpu.VMEM(block, BF16)] * owners
    else:
        me = jnp.zeros_like(me)
        shape = [jax.ShapeDtypeStruct((owners,) + block, BF16)]
    inputs = (
        trade_set.reshape(1, trades),
        set_slot.reshape(1, sets),
        trade_amounts,
        trade_legs,
        trade_loads,
    )
    packed = pl.pallas_call(
        lambda *refs: pack_kernel(owners, order, cap, set_count, *refs),
        out_shape=shape,
        in_specs=[smem()] + [pl.BlockSpec(memory_space=pltpu.HBM)] * 5,
        out_specs=vmem(len(shape)),
        scratch_shapes=[pltpu.VMEM(x.shape, x.dtype) for x in inputs] + [pltpu.SemaphoreType.DMA((5,))],
        compiler_params=params(),
        name="pack",
    )(me.reshape(1), *[pltpu.with_memory_space_constraint(x, pltpu.HBM) for x in inputs])
    states = path_states.reshape(cols, factors)
    reduced = pltpu.VMEM(((B + 1) * set_count, cols), F32)

    def scratch(batch):
        rows = batch * cap
        wide = -(-rows // 128) * 128
        return [
            pltpu.VMEM((rows, cols), F32),
            pltpu.VMEM((2 * wide, cols), BF16),
            pltpu.VMEM((wide, cols), BF16),
            pltpu.VMEM((wide, cols), BF16),
            pltpu.VMEM((B * set_count, 2 * wide), BF16),
        ]

    at, sofar = 0, []
    if few:
        got = [near(packed[0])] + [meet(packed[k], "trades", order[k]) for k in range(1, owners)]
        if owners > EARLY:
            at = EARLY
            sofar = pl.pallas_call(
                lambda *refs: add_kernel(cap, set_count, *refs),
                out_shape=[reduced],
                in_specs=vmem(1 + at),
                out_specs=vmem(1),
                scratch_shapes=scratch(at),
                compiler_params=params(),
                name="add",
            )(states, *got[:at])
            sofar = [near(sofar[0])]
        last, held = got[at:], owners - at
    else:
        last, held = [lax.all_to_all(packed[0], "trades", split_axis=0, concat_axis=0, tiled=True)], owners
    packet = (DATES * (set_count + NB) + NB + NB // 2, paths)
    mine, value = pl.pallas_call(
        lambda *refs: owner_kernel(owners, at, cap, set_count, *refs),
        out_shape=[
            pltpu.VMEM(packet, BF16),
            pltpu.VMEM((DATES, set_count, paths), F32),
        ],
        in_specs=vmem(2 + len(sofar) + len(last)),
        out_specs=vmem(2),
        scratch_shapes=scratch(held),
        compiler_params=params(),
        name="owner",
    )(near(risk_weights.reshape(1, B)), states, *sofar, *last)
    parts = [near(mine)] + [meet(mine, "paths", k) for k in range(1, groups)]
    fitted_margin, exposure = pl.pallas_call(
        lambda *refs: fit_kernel(groups, set_count, *refs),
        out_shape=[
            jax.ShapeDtypeStruct((DATES, set_count, paths), F32),
            jax.ShapeDtypeStruct((DATES, set_count), F32),
        ],
        in_specs=vmem(1 + groups),
        out_specs=vmem(2),
        compiler_params=params(),
        name="fit",
    )(near(value), *parts)
    return (fitted_margin, exposure)


def solution(mesh):
    in_specs = (
        P(None, "paths", None),
        P("trades", None),
        P(None, "trades"),
        P(None, "trades"),
        P("trades"),
        P(),
        P(),
    )
    out_specs = (P(None, "trades", "paths"), P(None, "trades"))
    return jax.shard_map(
        on_device, mesh=mesh, in_specs=in_specs, out_specs=out_specs, check_vma=False
    )
```
